128 devices in a mesh: dp: 16 (over x_hi, z, core), space: 8 (over y, x_lo).
Axes of the slice: x: 4 (x_hi: 2, x_lo: 2; x = x_hi * 2 + x_lo), y: 4, z: 4, core: 2. Of those that a mesh axis runs over, the one named last changes fastest.
Arguments:
- inputs: bfloat16 [16, 24, 32, 32, 256], P('dp', 'space'), may hold values from -6 to 6
- kernels: bfloat16 [2, 3, 3, 256, 256], P(None, None, None, 'dp'), may hold values from -0.125 to 0.125
- cotangent: bfloat16 [16, 24, 32, 32, 256], P('dp', 'space'), may hold values from -0.01171875 to 0.01171875
- adjacency: int32 [24, 4, 3], P('space'), may hold values from 0 to 23, as said below
Outputs:
- final_state: bfloat16 [16, 24, 32, 32, 256], P('dp', 'space')
- kernel_grads: float32 [2, 3, 3, 256, 256], P(None, None, None, 'dp')
The draws below stay inside these ranges and needn't reach their ends.
Inputs may be any that keep to these rules, and one draw needn't show every extreme that they name: Entry [t, e] = (n, f, r): edge e of tile t meets edge f of tile n, and r = 1 where the two edges are read in opposite directions along the shared line. The relation is symmetric: adjacency[n, f] = (t, e, r). The tiles form 2 x 2 blocks on the six faces of a cube, numbered in an order drawn from the seed.
All inputs are finite; a program needn't handle non-finite values.
Results may differ from the reference program's by a relative error of at most 0.005.
Values may be sent and summed in bfloat16 or wider, within the bound.
No kernel may reach another device: no remote copies, remote signals or barrier semaphores. Data moves between devices by JAX's collectives and lax.ppermute only.
A program may use at most 192 MiB of HBM per device.

```python
import jax
import jax.numpy as jnp
import numpy as np

C = 256
S = 32
FACE_SPLIT = 2
LAYERS = 2
TILES = 24
BATCH = 16


def vector_cross(first, second):
    return np.array([int(first[1]) * int(second[2]) - int(first[2]) * int(second[1]), int(first[2]) * int(second[0]) - int(first[0]) * int(second[2]), int(first[0]) * int(second[1]) - int(first[1]) * int(second[0])], np.int64)


def same_vector(first, second):
    return all((int(first[index]) == int(second[index]) for index in range(3)))


def edge_dirs(frame):
    normal, tangent_a, tangent_b = frame
    return [(-tangent_a, tangent_b), (tangent_a, tangent_b), (-tangent_b, tangent_a), (tangent_b, tangent_a)]


def cube_tables(split_num):
    frames = []
    for axis_num in range(3):
        for sign_val in (1, -1):
            normal = np.zeros(3, np.int64)
            normal[axis_num] = sign_val
            tangent_a = np.zeros(3, np.int64)
            tangent_a[(axis_num + 1) % 3] = 1
            tangent_b = vector_cross(normal, tangent_a)
            frames.append((normal, tangent_a, tangent_b))
    centers = {}
    for face_num in range(6):
        normal, tangent_a, tangent_b = frames[face_num]
        for row_num in range(split_num):
            for col_num in range(split_num):
                center_pt = split_num * normal + (2 * row_num + 1 - split_num) * tangent_a + (2 * col_num + 1 - split_num) * tangent_b
                centers[tuple((int(entry) for entry in center_pt))] = face_num * split_num * split_num + row_num * split_num + col_num
    tile_count = 6 * split_num * split_num
    neighbor = np.zeros((tile_count, 4), np.int64)
    facing = np.zeros((tile_count, 4), np.int64)
    reversal = np.zeros((tile_count, 4), np.int64)
    for face_num in range(6):
        normal, tangent_a, tangent_b = frames[face_num]
        directions = edge_dirs(frames[face_num])
        for row_num in range(split_num):
            for col_num in range(split_num):
                position = face_num * split_num * split_num + row_num * split_num + col_num
                center_pt = split_num * normal + (2 * row_num + 1 - split_num) * tangent_a + (2 * col_num + 1 - split_num) * tangent_b
                for edge_num in range(4):
                    outward, along_dir = directions[edge_num]
                    step_row = row_num + (-1 if edge_num == 0 else 1 if edge_num == 1 else 0)
                    step_col = col_num + (-1 if edge_num == 2 else 1 if edge_num == 3 else 0)
                    if 0 <= step_row < split_num and 0 <= step_col < split_num:
                        neighbor[position, edge_num] = face_num * split_num * split_num + step_row * split_num + step_col
                        facing[position, edge_num] = edge_num ^ 1
                        reversal[position, edge_num] = 0
                    else:
                        across_pt = center_pt + outward - normal
                        across = centers[tuple((int(entry) for entry in across_pt))]
                        across_face = across // (split_num * split_num)
                        across_dirs = edge_dirs(frames[across_face])
                        back_edge = [candidate for candidate in range(4) if same_vector(across_dirs[candidate][0], -normal)][0]
                        neighbor[position, edge_num] = across
                        facing[position, edge_num] = back_edge
                        reversal[position, edge_num] = 0 if same_vector(across_dirs[back_edge][1], along_dir) else 1
    return np.stack([neighbor, facing, reversal], axis=2)


def draw_adjacency(key, part):
    table = jnp.asarray(cube_tables(FACE_SPLIT), jnp.int32)
    shuffled = jax.random.permutation(key, 6 * FACE_SPLIT * FACE_SPLIT).astype(jnp.int32)
    positions = jnp.argsort(shuffled).astype(jnp.int32)
    rows_here = table[positions]
    return jnp.stack([shuffled[rows_here[:, :, 0]], rows_here[:, :, 1], rows_here[:, :, 2]], axis=2).astype(jnp.int32)


def shard_levels(stream_key, shape, shards, least, largest):
    def one(dim, shards_of):
        steps = jax.random.uniform(jax.random.fold_in(jax.random.fold_in(stream_key, 6), dim), (shards_of,), jnp.float32, least / len(shards), largest / len(shards))
        return jnp.repeat(jnp.exp(steps), shape[dim] // shards_of).reshape((-1,) + (1,) * (len(shape) - dim - 1))

    level = one(*shards[0])
    for cut in shards[1:]:
        level = level * one(*cut)
    return level


def centred(rng, dims, deviation, reach, shards=(), held_as=jnp.bfloat16):
    factor_of = shard_levels(rng, dims, shards, -0.22, 0.18) if shards else 1.0
    entries = jax.random.normal(rng, dims, jnp.float32) * deviation * factor_of
    return jnp.minimum(jnp.maximum(entries, -reach), reach).astype(held_as)


def setup_inputs(seed: int = 0) -> dict:
    seeds = jax.random.split(jax.random.key(seed), 5)
    inputs = centred(seeds[0], (BATCH, TILES, S, S, C), 1.0, 6.0, ((0, 16), (1, 8)))
    kernels = centred(seeds[1], (LAYERS, 3, 3, C, C), (9 * C) ** -0.5, 0.125, ((3, 16),))
    cotangent = centred(seeds[2], (BATCH, TILES, S, S, C), 0.002, 0.01171875, ((0, 16), (1, 8)))
    adjacency = draw_adjacency(jax.random.fold_in(seeds[4], 71), 0)
    return {"inputs": inputs, "kernels": kernels, "cotangent": cotangent, "adjacency": adjacency}


def edge_strips(tile_field):
    return jnp.stack([tile_field[:, :, 0], tile_field[:, :, -1], tile_field[:, :, :, 0], tile_field[:, :, :, -1]], axis=2)

def orient(strips, adjacency):
    selected = strips[:, adjacency[:, :, 0], adjacency[:, :, 1]]
    flipped = (adjacency[:, :, 2] == 1)[None, :, :, None, None]
    return jnp.where(flipped, selected[:, :, :, ::-1], selected)

def with_rim(tile_field, rim_rows):
    padded = jnp.pad(tile_field, ((0, 0), (0, 0), (1, 1), (1, 1), (0, 0)))
    padded = padded.at[:, :, 0, 1:-1].set(rim_rows[:, :, 0])
    padded = padded.at[:, :, -1, 1:-1].set(rim_rows[:, :, 1])
    padded = padded.at[:, :, 1:-1, 0].set(rim_rows[:, :, 2])
    padded = padded.at[:, :, 1:-1, -1].set(rim_rows[:, :, 3])
    return padded

def convolve(padded, kernel):
    extent = padded.shape[2] - 2
    channels = padded.shape[-1]
    summed = jnp.zeros(padded.shape[:2] + (extent, extent, kernel.shape[-1]), jnp.float32)
    for row_off in range(3):
        for col_off in range(3):
            patches = padded[:, :, row_off:row_off + extent, col_off:col_off + extent].reshape(-1, channels)
            summed = summed + jnp.dot(patches, kernel[row_off, col_off], preferred_element_type=jnp.float32).reshape(summed.shape)
    return summed

def weight_grad(padded, flat_grad):
    extent = padded.shape[2] - 2
    channels = padded.shape[-1]
    rows_out = []
    for row_off in range(3):
        row_list = []
        for col_off in range(3):
            patches = padded[:, :, row_off:row_off + extent, col_off:col_off + extent].reshape(-1, channels)
            row_list.append(jnp.dot(patches.T, flat_grad, preferred_element_type=jnp.float32))
        rows_out.append(jnp.stack(row_list))
    return jnp.stack(rows_out)

def input_grad(flat_grad, kernel, padded_shape):
    extent = padded_shape[2] - 2
    pad_grad = jnp.zeros(padded_shape, jnp.float32)
    piece_shape = padded_shape[:2] + (extent, extent, padded_shape[4])
    for row_off in range(3):
        for col_off in range(3):
            contrib = jnp.dot(flat_grad, kernel[row_off, col_off].T, preferred_element_type=jnp.float32).reshape(piece_shape)
            pad_grad = pad_grad.at[:, :, row_off:row_off + extent, col_off:col_off + extent].add(contrib)
    return pad_grad

def rim_strips(pad_grad):
    return jnp.stack([pad_grad[:, :, 0, 1:-1], pad_grad[:, :, -1, 1:-1], pad_grad[:, :, 1:-1, 0], pad_grad[:, :, 1:-1, -1]], axis=2)

def add_rim(interior, returned):
    interior = interior.at[:, :, 0].add(returned[:, :, 0])
    interior = interior.at[:, :, -1].add(returned[:, :, 1])
    interior = interior.at[:, :, :, 0].add(returned[:, :, 2])
    interior = interior.at[:, :, :, -1].add(returned[:, :, 3])
    return interior

def reference(inputs, kernels, cotangent, adjacency):
    current = inputs
    stored = []
    for layer_num in range(LAYERS):
        rim_rows = orient(edge_strips(current), adjacency)
        padded = with_rim(current, rim_rows)
        preact = convolve(padded, kernels[layer_num])
        current = (current.astype(jnp.float32) + jax.nn.silu(preact)).astype(jnp.bfloat16)
        stored.append((padded, preact))
    upstream = cotangent.astype(jnp.float32)
    kernel_grads = [None] * LAYERS
    for layer_num in range(LAYERS - 1, -1, -1):
        padded, preact = stored[layer_num]
        logistic = jax.nn.sigmoid(preact)
        pre_grad = (upstream * logistic * (1.0 + preact * (1.0 - logistic))).astype(jnp.bfloat16)
        flat_grad = pre_grad.reshape(-1, pre_grad.shape[-1])
        kernel_grads[layer_num] = weight_grad(padded, flat_grad)
        if layer_num > 0:
            pad_grad = input_grad(flat_grad, kernels[layer_num], padded.shape)
            rim_values = rim_strips(pad_grad).astype(jnp.bfloat16)
            returned = orient(rim_values, adjacency).astype(jnp.float32)
            upstream = add_rim(upstream + pad_grad[:, :, 1:-1, 1:-1], returned)
    return (current, jnp.stack(kernel_grads))
```

```python
import jax
import jax.numpy as jnp
from jax import lax
from jax.experimental import pallas as pl
from jax.experimental.pallas import tpu as pltpu
from jax.sharding import PartitionSpec as P

BF = jnp.bfloat16
F32 = jnp.float32
TILES, SIDE, CH = 3, 32, 256
CELLS = SIDE * SIDE
SLOTS = 7
GOT, BACK = 64, 76


def vmem():
    return pl.BlockSpec(memory_space=pltpu.VMEM)


def smem():
    return pl.BlockSpec(memory_space=pltpu.SMEM)


def whole(shape):
    zeros = (0,) * len(shape)
    return pl.BlockSpec(shape, lambda t: zeros)


def per_tile(*tail):
    zeros = (0,) * (len(tail) - 1)
    return pl.BlockSpec(tail, lambda t: (t, *zeros))


def struct(shape, dtype):
    return jax.ShapeDtypeStruct(shape, dtype)


def params(steps=0):
    if steps:
        return pltpu.CompilerParams(
            dimension_semantics=("arbitrary",), vmem_limit_bytes=60 * 1024 * 1024
        )
    return pltpu.CompilerParams(vmem_limit_bytes=60 * 1024 * 1024)


def cost(flops, moved):
    return pl.CostEstimate(flops=flops, bytes_accessed=moved, transcendentals=0)


def take(halves, rows):
    return jnp.concatenate([halves[0, rows, :], halves[1, rows, :]], axis=1)


def put(halves, rows, value):
    halves[0, rows, :] = value[:, 0:128]
    halves[1, rows, :] = value[:, 128:256]


def fill(routes_ref, strips, send_ref):
    for slot in range(send_ref.shape[0]):
        send_ref[slot] = strips[routes_ref[slot]]


def pack_kernel(me_ref, adj_ref, field_ref, send_ref, routes_ref, column, strips):
    peers = adj_ref.shape[0]
    me = me_ref[0]
    for slot in range(GOT):
        routes_ref[slot] = 0
    for peer in range(peers):
        sent = jnp.int32(0)
        for edge in range(4 * TILES):
            other = adj_ref[peer, edge * 3]
            owner = lax.div(other, TILES)
            mine = (owner == me).astype(jnp.int32)
            slot = peer * SLOTS + jnp.minimum(sent, SLOTS - 1)
            strip = (other - owner * TILES) * 4 + adj_ref[peer, edge * 3 + 1]
            routes_ref[jnp.where(owner == me, slot, GOT - 1)] = jnp.where(owner == me, strip, 0)
            sent += mine
    owners = []
    for edge in range(4 * TILES):
        owners.append(lax.div(adj_ref[me, edge * 3], TILES))
        before = jnp.int32(0)
        for there in range(edge):
            before += (owners[there] == owners[edge]).astype(jnp.int32)
        routes_ref[GOT + edge] = owners[edge] * SLOTS + jnp.minimum(before, SLOTS - 1)
        routes_ref[BACK + edge] = adj_ref[me, edge * 3 + 2]
    for tile in range(TILES):
        strips[tile * 4] = field_ref[tile, 0]
        strips[tile * 4 + 1] = field_ref[tile, SIDE - 1]
        for edge, first, lane in ((2, 0, 0), (3, SIDE - 8, 7)):
            near = field_ref[tile, :, first : first + 8].astype(F32).reshape(SIDE * 8, CH)
            put(column, slice(None), near)
            strips[tile * 4 + edge] = take(column, pl.ds(lane, SIDE, stride=8)).astype(BF)
    fill(routes_ref, strips, send_ref)


def pack(me, adjacency, field):
    peers = adjacency.shape[0]
    return pl.pallas_call(
        pack_kernel,
        name="pack",
        out_shape=(struct((peers * SLOTS, SIDE, CH), BF), struct((BACK + 12,), jnp.int32)),
        in_specs=[smem(), smem(), vmem()],
        out_specs=(vmem(), smem()),
        scratch_shapes=[
            pltpu.VMEM((2, SIDE * 8, 128), F32),
            pltpu.VMEM((4 * TILES, SIDE, CH), BF),
        ],
        compiler_params=params(),
        cost_estimate=cost(0, 3_000_000),
    )(me, adjacency, field)


def pick(rows, shift_of_block, backwards):
    row = lax.broadcasted_iota(jnp.int32, (rows, SIDE), 0)
    cell = lax.broadcasted_iota(jnp.int32, (rows, SIDE), 1)
    block = row // SIDE
    place = row - block * SIDE
    source = place + shift_of_block(block)
    inside = (source >= 0) & (source < SIDE)
    if backwards is not None:
        source = jnp.where(backwards == 1, SIDE - 1 - source, source)
    return jnp.where(inside & (cell == source), 1.0, 0.0).astype(BF)


def dot(left, right):
    return jnp.dot(left, right, preferred_element_type=F32)


def dot_rows(left, right):
    return lax.dot_general(left, right, (((0,), (0,)), ((), ())), preferred_element_type=F32)


def block_of_edge(edge, k):
    return (k, 6 + k, 3 * k, 3 * k + 2)[edge]


EDGE_ROWS = (
    pl.ds(0, SIDE),
    pl.ds(CELLS - SIDE, SIDE),
    pl.ds(0, SIDE, stride=SIDE),
    pl.ds(SIDE - 1, SIDE, stride=SIDE),
)


def spread(source, out_ref, ascending):
    first = lax.broadcasted_iota(jnp.int32, (SIDE, CH), 0) == 0
    last = lax.broadcasted_iota(jnp.int32, (SIDE, CH), 0) == SIDE - 1

    def one(i, carry):
        row = source(i).astype(F32)
        earlier = jnp.where(first, 0.0, pltpu.roll(row, 1, 0)).astype(BF)
        later = jnp.where(last, 0.0, pltpu.roll(row, SIDE - 1, 0)).astype(BF)
        at = pl.ds(pl.multiple_of((i + 1) * SIDE, SIDE), SIDE)
        low, high = (earlier, later) if ascending else (later, earlier)
        out_ref[at, 0:CH] = low
        out_ref[at, CH : 2 * CH] = row.astype(BF)
        out_ref[at, 2 * CH : 3 * CH] = high
        return carry

    lax.fori_loop(0, SIDE, one, 0, unroll=4)


def clear_margin(out_ref):
    zero = jnp.zeros((SIDE, 3 * CH), BF)
    out_ref[0:SIDE, :] = zero
    out_ref[CELLS + SIDE : CELLS + 2 * SIDE, :] = zero


def conv_kernel(turned, shards, core_ref, field_ref, mine_ref, theirs_ref, *refs):
    if turned:
        part_ref, kernel_ref, turned_ref, wide = refs
    else:
        part_ref, kernel_ref, wide = refs
    depth = CH // shards
    core = core_ref[0]

    @pl.when(pl.program_id(0) == 0)
    def _():
        clear_margin(wide)
        for pair in range(shards // 2):
            for source, side in ((mine_ref, core), (theirs_ref, 1 - core)):
                for tap in range(9):
                    at = pl.multiple_of(tap * CH + pair * 2 * depth + side * depth, depth)
                    kernel_ref[pl.ds(at, depth), :] = source[pair, 0, tap]
        if turned:
            for tap in range(9):
                turned_ref[tap * CH : (tap + 1) * CH, :] = kernel_ref[tap * CH : (tap + 1) * CH, :].T

    spread(lambda i: field_ref[0, i], wide, True)

    def chunk(c, carry):
        total = None
        for p in range(3):
            at = pl.multiple_of(c * CH + p * SIDE, SIDE)
            term = dot(wide[pl.ds(at, CH), :], kernel_ref[p * 3 * CH : (p + 1) * 3 * CH, :])
            total = term if total is None else total + term
        part_ref[pl.ds(pl.multiple_of(c * CH, CH), CH), :] = total
        return carry

    lax.fori_loop(0, CELLS // CH, chunk, 0)


def conv(core, field, mine, theirs, layer, turned):
    pieces = pl.BlockSpec((mine.shape[0], 1, *mine.shape[2:]), lambda t: (0, layer, 0, 0, 0))
    shards = mine.shape[0] * 2
    outs = [struct((TILES * CELLS, CH), F32), struct((9 * CH, CH), BF)]
    specs = [per_tile(CELLS, CH), whole((9 * CH, CH))]
    if turned:
        outs.append(struct((9 * CH, CH), BF))
        specs.append(whole((9 * CH, CH)))
    return pl.pallas_call(
        lambda *refs: conv_kernel(turned, shards, *refs),
        name="conv_turned" if turned else "conv",
        out_shape=tuple(outs),
        grid=(TILES,),
        in_specs=[smem(), per_tile(1, SIDE, SIDE, CH), pieces, pieces],
        out_specs=tuple(specs),
        scratch_shapes=[pltpu.VMEM((CELLS + 2 * SIDE, 3 * CH), BF)],
        compiler_params=params(1),
        cost_estimate=cost(3_600_000_000, 7_000_000),
    )(core, field, mine, theirs)


def add_rims(routes_ref, got_ref, kernel_ref, rows3, rim_part):
    for edge in range(4):
        for tile in range(TILES):
            back = routes_ref[BACK + tile * 4 + edge]
            choose = pick(3 * SIDE, lambda block: block - 1, back)
            shifted = dot(choose, got_ref[routes_ref[GOT + tile * 4 + edge]]).astype(BF)
            for k in range(3):
                rows3[tile * SIDE : (tile + 1) * SIDE, k * CH : (k + 1) * CH] = shifted[
                    k * SIDE : (k + 1) * SIDE
                ]
        total = None
        for k in range(3):
            block = block_of_edge(edge, k)
            term = dot(
                rows3[:, k * CH : (k + 1) * CH], kernel_ref[block * CH : (block + 1) * CH, :]
            )
            total = term if total is None else total + term
        rim_part[edge] = total


def with_rims(part_ref, rim_part, out):
    tile = pl.program_id(0)
    put(out, slice(None), part_ref[...])
    for edge in range(4):
        rows = EDGE_ROWS[edge]
        add = rim_part[edge, pl.ds(pl.multiple_of(tile * SIDE, SIDE), SIDE), :]
        put(out, rows, take(out, rows) + add)


def finish_kernel(
    routes_ref,
    part_ref,
    field_ref,
    got_ref,
    kernel_ref,
    state_ref,
    slope_ref,
    send_ref,
    rows3,
    rim_part,
    fresh,
    strips,
):
    tile = pl.program_id(0)

    @pl.when(tile == 0)
    def _():
        add_rims(routes_ref, got_ref, kernel_ref, rows3, rim_part)

    with_rims(part_ref, rim_part, fresh)

    def one(i, carry):
        at = pl.ds(pl.multiple_of(i * SIDE, SIDE), SIDE)
        v = take(fresh, at)
        s = 1.0 / (1.0 + jnp.exp(-v))
        updated = field_ref[0, i].astype(F32) + v * s
        put(fresh, at, updated)
        state_ref[0, i] = updated.astype(BF)
        slope_ref[at, :] = s * (1.0 + v * (1.0 - s))
        return carry

    lax.fori_loop(0, SIDE, one, 0, unroll=4)
    for edge in range(4):
        strips[tile * 4 + edge] = take(fresh, EDGE_ROWS[edge]).astype(BF)

    @pl.when(tile == TILES - 1)
    def _():
        fill(routes_ref, strips, send_ref)


def finish(routes, part, field, got, kernel):
    return pl.pallas_call(
        finish_kernel,
        name="finish",
        out_shape=(
            struct(field.shape, BF),
            struct(part.shape, F32),
            struct(got.shape, BF),
        ),
        grid=(TILES,),
        in_specs=[
            smem(),
            per_tile(CELLS, CH),
            per_tile(1, SIDE, SIDE, CH),
            whole(got.shape),
            whole(kernel.shape),
        ],
        out_specs=(per_tile(1, SIDE, SIDE, CH), per_tile(CELLS, CH), whole(got.shape)),
        scratch_shapes=[
            pltpu.VMEM((TILES * SIDE, 3 * CH), BF),
            pltpu.VMEM((4, TILES * SIDE, CH), F32),
            pltpu.VMEM((2, CELLS, 128), F32),
            pltpu.VMEM((4 * TILES, SIDE, CH), BF),
        ],
        compiler_params=params(1),
        cost_estimate=cost(200_000_000, 10_000_000),
    )(routes, part, field, got, kernel)


def note_strips(grad, triples, tile):
    choose = pick(3 * SIDE, lambda block: 1 - block, None)
    for edge in range(4):
        shifted = dot(choose, take(grad, EDGE_ROWS[edge]).astype(BF)).astype(BF)
        for k in range(3):
            triples[
                edge, pl.ds(pl.multiple_of(tile * SIDE, SIDE), SIDE), k * CH : (k + 1) * CH
            ] = shifted[k * SIDE : (k + 1) * SIDE]


def last_kernel(
    routes_ref,
    part_ref,
    field_ref,
    got_ref,
    kernel_ref,
    turned_ref,
    cot_ref,
    state_ref,
    grad_ref,
    send_ref,
    triples_ref,
    rows3,
    rim_part,
    fresh,
    strips,
):
    tile = pl.program_id(0)

    @pl.when(tile == 0)
    def _():
        add_rims(routes_ref, got_ref, kernel_ref, rows3, rim_part)

    with_rims(part_ref, rim_part, fresh)

    def one(i, carry):
        at = pl.ds(pl.multiple_of(i * SIDE, SIDE), SIDE)
        v = take(fresh, at)
        s = 1.0 / (1.0 + jnp.exp(-v))
        state_ref[0, i] = (field_ref[0, i].astype(F32) + v * s).astype(BF)
        grad = cot_ref[0, i].astype(F32) * s * (1.0 + v * (1.0 - s))
        put(fresh, at, grad)
        grad_ref[at, :] = grad.astype(BF)
        return carry

    lax.fori_loop(0, SIDE, one, 0, unroll=4)
    note_strips(fresh, triples_ref, tile)

    @pl.when(tile == TILES - 1)
    def _():
        for edge in range(4):
            total = None
            for k in range(3):
                block = block_of_edge(edge, k)
                term = dot(
                    triples_ref[edge, :, k * CH : (k + 1) * CH],
                    turned_ref[block * CH : (block + 1) * CH, :],
                )
                total = term if total is None else total + term
            for there in range(TILES):
                strips[there * 4 + edge] = total[there * SIDE : (there + 1) * SIDE].astype(BF)
        fill(routes_ref, strips, send_ref)


def last(routes, part, field, got, kernel, turned, cotangent):
    triples = (4, TILES * SIDE, 3 * CH)
    return pl.pallas_call(
        last_kernel,
        name="last",
        out_shape=(
            struct(field.shape, BF),
            struct((TILES * CELLS, CH), BF),
            struct(got.shape, BF),
            struct(triples, BF),
        ),
        grid=(TILES,),
        in_specs=[
            smem(),
            per_tile(CELLS, CH),
            per_tile(1, SIDE, SIDE, CH),
            whole(got.shape),
            whole(kernel.shape),
            whole(turned.shape),
            per_tile(1, SIDE, SIDE, CH),
        ],
        out_specs=(
            per_tile(1, SIDE, SIDE, CH),
            per_tile(CELLS, CH),
            whole(got.shape),
            whole(triples),
        ),
        scratch_shapes=[
            pltpu.VMEM((TILES * SIDE, 3 * CH), BF),
            pltpu.VMEM((4, TILES * SIDE, CH), F32),
            pltpu.VMEM((2, CELLS, 128), F32),
            pltpu.VMEM((4 * TILES, SIDE, CH), BF),
        ],
        compiler_params=params(1),
        cost_estimate=cost(400_000_000, 12_000_000),
    )(routes, part, field, got, kernel, turned, cotangent)


def outer(field, wide, across, total):
    across[...] = field.reshape(CELLS, CH).T

    def one(p, carry):
        at = pl.multiple_of((2 - p) * SIDE, SIDE)
        total[p] = total[p] + dot(across[...], wide[pl.ds(at, CELLS), :])
        return carry

    lax.fori_loop(0, 3, one, 0)


def outer_rims(routes_ref, got_ref, triples, total, flat):
    for edge in range(4):
        for tile in range(TILES):
            back = routes_ref[BACK + tile * 4 + edge]
            choose = pick(SIDE, lambda block: 0, back)
            flat[tile * SIDE : (tile + 1) * SIDE, :] = dot(
                choose, got_ref[routes_ref[GOT + tile * 4 + edge]]
            ).astype(BF)
        for k in range(3):
            p, q = divmod(block_of_edge(edge, k), 3)
            lanes = slice(q * CH, (q + 1) * CH)
            total[p, :, lanes] = total[p, :, lanes] + dot_rows(
                flat[...], triples[edge, :, k * CH : (k + 1) * CH]
            )


def hand_over(core, total, kept_ref, given_ref):
    pairs = kept_ref.shape[0]
    depth = kept_ref.shape[2]
    for pair in range(pairs):
        own = pl.ds(pl.multiple_of(pair * 2 * depth + core * depth, depth), depth)
        other = pl.ds(pl.multiple_of(pair * 2 * depth + (1 - core) * depth, depth), depth)
        for tap in range(9):
            p, q = divmod(tap, 3)
            kept_ref[pair, tap] = total[p, own, q * CH : (q + 1) * CH]
            given_ref[pair, tap] = total[p, other, q * CH : (q + 1) * CH].astype(BF)


def second_kernel(
    routes_ref,
    core_ref,
    field_ref,
    grad_ref,
    got_ref,
    triples_ref,
    turned_ref,
    back_ref,
    kept_ref,
    given_ref,
    wide,
    across,
    total,
    flat,
):
    tile = pl.program_id(0)

    @pl.when(tile == 0)
    def _():
        clear_margin(wide)
        total[...] = jnp.zeros_like(total)

    spread(lambda i: grad_ref[pl.ds(pl.multiple_of(i * SIDE, SIDE), SIDE), :], wide, False)

    def chunk(c, carry):
        result = None
        for p in range(3):
            at = pl.multiple_of(c * CH + (2 - p) * SIDE, SIDE)
            term = dot(wide[pl.ds(at, CH), :], turned_ref[p * 3 * CH : (p + 1) * 3 * CH, :])
            result = term if result is None else result + term
        back_ref[pl.ds(pl.multiple_of(c * CH, CH), CH), :] = result
        return carry

    lax.fori_loop(0, CELLS // CH, chunk, 0)
    outer(field_ref[0], wide, across, total)

    @pl.when(tile == TILES - 1)
    def _():
        outer_rims(routes_ref, got_ref, triples_ref, total, flat)
        hand_over(core_ref[0], total, kept_ref, given_ref)


def second(routes, core, field, grad, got, triples, turned, pairs, depth):
    half = (pairs, 9, depth, CH)
    return pl.pallas_call(
        second_kernel,
        name="second",
        out_shape=(struct((TILES * CELLS, CH), F32), struct(half, F32), struct(half, BF)),
        grid=(TILES,),
        in_specs=[
            smem(),
            smem(),
            per_tile(1, SIDE, SIDE, CH),
            per_tile(CELLS, CH),
            whole(got.shape),
            whole(triples.shape),
            whole(turned.shape),
        ],
        out_specs=(per_tile(CELLS, CH), whole(half), whole(half)),
        scratch_shapes=[
            pltpu.VMEM((CELLS + 2 * SIDE, 3 * CH), BF),
            pltpu.VMEM((CH, CELLS), BF),
            pltpu.VMEM((3, CH, 3 * CH), F32),
            pltpu.VMEM((TILES * SIDE, CH), BF),
        ],
        compiler_params=params(1),
        cost_estimate=cost(7_200_000_000, 12_000_000),
    )(routes, core, field, grad, got, triples, turned)


def first_kernel(
    routes_ref,
    core_ref,
    field_ref,
    cot_ref,
    back_ref,
    slope_ref,
    got_ref,
    returned_ref,
    kept_ref,
    given_ref,
    wide,
    across,
    total,
    flat,
    fresh,
    triples,
):
    tile = pl.program_id(0)

    @pl.when(tile == 0)
    def _():
        clear_margin(wide)
        total[...] = jnp.zeros_like(total)

    def one(i, carry):
        at = pl.ds(pl.multiple_of(i * SIDE, SIDE), SIDE)
        put(fresh, at, cot_ref[0, i].astype(F32) + back_ref[at, :])
        return carry

    lax.fori_loop(0, SIDE, one, 0, unroll=4)
    for edge in range(4):
        back = routes_ref[BACK + tile * 4 + edge]
        choose = pick(SIDE, lambda block: 0, back)
        rows = EDGE_ROWS[edge]
        add = dot(choose, returned_ref[routes_ref[GOT + tile * 4 + edge]])
        put(fresh, rows, take(fresh, rows) + add)

    def two(i, carry):
        at = pl.ds(pl.multiple_of(i * SIDE, SIDE), SIDE)
        put(fresh, at, take(fresh, at) * slope_ref[at, :])
        return carry

    lax.fori_loop(0, SIDE, two, 0, unroll=4)
    note_strips(fresh, triples, tile)
    spread(lambda i: take(fresh, pl.ds(pl.multiple_of(i * SIDE, SIDE), SIDE)), wide, False)
    outer(field_ref[0], wide, across, total)

    @pl.when(tile == TILES - 1)
    def _():
        outer_rims(routes_ref, got_ref, triples, total, flat)
        hand_over(core_ref[0], total, kept_ref, given_ref)


def first(routes, core, field, cotangent, back, slope, got, returned, pairs, depth):
    half = (pairs, 9, depth, CH)
    return pl.pallas_call(
        first_kernel,
        name="first",
        out_shape=(struct(half, F32), struct(half, BF)),
        grid=(TILES,),
        in_specs=[
            smem(),
            smem(),
            per_tile(1, SIDE, SIDE, CH),
            per_tile(1, SIDE, SIDE, CH),
            per_tile(CELLS, CH),
            per_tile(CELLS, CH),
            whole(got.shape),
            whole(returned.shape),
        ],
        out_specs=(whole(half), whole(half)),
        scratch_shapes=[
            pltpu.VMEM((CELLS + 2 * SIDE, 3 * CH), BF),
            pltpu.VMEM((CH, CELLS), BF),
            pltpu.VMEM((3, CH, 3 * CH), F32),
            pltpu.VMEM((TILES * SIDE, CH), BF),
            pltpu.VMEM((2, CELLS, 128), F32),
            pltpu.VMEM((4, TILES * SIDE, 3 * CH), BF),
        ],
        compiler_params=params(1),
        cost_estimate=cost(3_600_000_000, 12_000_000),
    )(routes, core, field, cotangent, back, slope, got, returned)


def cut_kernel(kept_ref, got_ref, out_ref, rows):
    pairs, _, depth, _ = kept_ref.shape
    run = 9 * depth // 4
    for pair in range(pairs):
        for tap in range(9):
            rows[tap * depth : (tap + 1) * depth, :] = kept_ref[pair, tap] + got_ref[
                pair, tap
            ].astype(F32)
        for peer in range(8):
            high, low = divmod(peer, 4)
            out_ref[pair * 8 + peer] = rows[
                low * run : (low + 1) * run, high * 128 : (high + 1) * 128
            ].astype(BF)


def cut(kept, got):
    pairs, _, depth, _ = kept.shape
    return pl.pallas_call(
        cut_kernel,
        name="cut",
        out_shape=struct((pairs * 8, 9 * depth // 4, 128), BF),
        in_specs=[vmem(), vmem()],
        out_specs=vmem(),
        scratch_shapes=[pltpu.VMEM((9 * depth, CH), F32)],
        compiler_params=params(),
        cost_estimate=cost(0, 3_000_000),
    )(kept, got)


def sum_kernel(*refs):
    *in_refs, out_ref = refs
    for layer, source in enumerate(in_refs):
        summed = source[0].astype(F32)
        for other in range(1, source.shape[0]):
            summed = summed + source[other].astype(F32)
        for peer in range(out_ref.shape[0]):
            run = summed.shape[0]
            out_ref[peer, layer * run : (layer + 1) * run] = summed


def sum_all(parts, peers):
    return pl.pallas_call(
        sum_kernel,
        name="sum_all",
        out_shape=struct((peers, len(parts) * parts[0].shape[1], 128), F32),
        in_specs=[vmem()] * len(parts),
        out_specs=vmem(),
        compiler_params=params(),
        cost_estimate=cost(0, 2_000_000),
    )(*parts)


def join_kernel(in_ref, out_ref):
    peers = in_ref.shape[0]
    run = in_ref.shape[1] // 2
    rows_all = out_ref.shape[0] // 2
    for layer in range(2):
        for peer in range(peers):
            high, low = divmod(peer, 4)
            at = layer * rows_all + low * run
            out_ref[at : at + run, high * 128 : (high + 1) * 128] = in_ref[
                peer, layer * run : (layer + 1) * run
            ]


def join(blocks, depth):
    return pl.pallas_call(
        join_kernel,
        name="join",
        out_shape=struct((2 * 9 * depth, CH), F32),
        in_specs=[vmem()],
        out_specs=vmem(),
        compiler_params=params(),
        cost_estimate=cost(0, 600_000),
    )(blocks)


def exchange(value, axes, groups=None):
    return lax.all_to_all(value, axes, 0, 0, tiled=True, axis_index_groups=groups)


def solution(mesh):
    shards, peers = mesh.shape["dp"], mesh.shape["space"]
    pairs, depth = shards // 2, CH // shards
    same_core = [[pair * 2 + core for pair in range(pairs)] for core in range(2)]
    same_core_all = [
        [(pair * 2 + core) * peers + peer for pair in range(pairs) for peer in range(peers)]
        for core in range(2)
    ]
    swap = [(index, index ^ 1) for index in range(shards)]

    def gather(shard):
        mine = exchange(
            jnp.broadcast_to(shard[None], (pairs, *shard.shape)), "dp", same_core
        )
        return mine, lax.ppermute(mine, "dp", swap)

    def trade(strips):
        return exchange(strips.reshape(peers, SLOTS, SIDE, CH), "space").reshape(strips.shape)

    def halve(kept, given):
        return cut(kept, lax.ppermute(given, "dp", swap))

    def per_device(inputs, kernels, cotangent, adjacency):
        field = inputs[0]
        cot = cotangent[0]
        core = (lax.axis_index("dp") % 2).astype(jnp.int32).reshape(1)
        me = lax.axis_index("space").astype(jnp.int32).reshape(1)
        edges = exchange(jnp.broadcast_to(adjacency.reshape(1, 36), (peers, 36)), "space")
        taps = kernels.reshape(2, 9, depth, CH)
        mine, theirs = gather(taps)
        send1, routes = pack(me, edges, field)
        got1 = trade(send1)
        part1, kernel1 = conv(core, field, mine, theirs, 0, False)
        state1, slope1, send2 = finish(routes, part1, field, got1, kernel1)
        got2 = trade(send2)
        part2, kernel2, turned2 = conv(core, state1, mine, theirs, 1, True)
        state2, grad2, send3, triples2 = last(routes, part2, state1, got2, kernel2, turned2, cot)
        returned = trade(send3)
        back, kept2, given2 = second(
            routes, core, state1, grad2, got2, triples2, turned2, pairs, depth
        )
        blocks2, back = lax.optimization_barrier((halve(kept2, given2), back))
        layer2 = exchange(blocks2, ("dp", "space"), same_core_all)
        kept1, given1 = first(routes, core, field, cot, back, slope1, got1, returned, pairs, depth)
        layer1 = exchange(halve(kept1, given1), ("dp", "space"), same_core_all)
        summed = sum_all((layer1, layer2), peers)
        grads = join(exchange(summed, "space"), depth)
        return state2[None], grads.reshape(2, 3, 3, depth, CH)

    in_specs = (
        P("dp", "space", None, None, None),
        P(None, None, None, "dp", None),
        P("dp", "space", None, None, None),
        P("space", None, None),
    )
    out_specs = (P("dp", "space", None, None, None), P(None, None, None, "dp", None))
    return jax.shard_map(
        per_device, mesh=mesh, in_specs=in_specs, out_specs=out_specs, check_vma=False
    )
```

```python
import jax
import jax.numpy as jnp
from jax import lax
from jax.experimental import pallas as pl
from jax.experimental.pallas import tpu as pltpu
from jax.sharding import PartitionSpec as P

BF = jnp.bfloat16
F32 = jnp.float32
TILES, SIDE, CH = 3, 32, 256
CELLS = SIDE * SIDE
SLOTS = 7
GOT, BACK = 64, 76


def vmem():
    return pl.BlockSpec(memory_space=pltpu.VMEM)


def smem():
    return pl.BlockSpec(memory_space=pltpu.SMEM)


def whole(shape):
    zeros = (0,) * len(shape)
    return pl.BlockSpec(shape, lambda t: zeros)


def per_tile(*tail):
    zeros = (0,) * (len(tail) - 1)
    return pl.BlockSpec(tail, lambda t: (t, *zeros))


def struct(shape, dtype):
    return jax.ShapeDtypeStruct(shape, dtype)


def params(steps=0):
    if steps:
        return pltpu.CompilerParams(
            dimension_semantics=("arbitrary",), vmem_limit_bytes=60 * 1024 * 1024
        )
    return pltpu.CompilerParams(vmem_limit_bytes=60 * 1024 * 1024)


def cost(flops, moved):
    return pl.CostEstimate(flops=flops, bytes_accessed=moved, transcendentals=0)


def take(halves, rows):
    return jnp.concatenate([halves[0, rows, :], halves[1, rows, :]], axis=1)


def put(halves, rows, value):
    halves[0, rows, :] = value[:, 0:128]
    halves[1, rows, :] = value[:, 128:256]


def fill(routes_ref, strips, send_ref):
    for slot in range(send_ref.shape[0]):
        send_ref[slot] = strips[routes_ref[slot]]


def pack_kernel(me_ref, adj_ref, field_ref, send_ref, routes_ref, column, strips):
    peers = adj_ref.shape[0]
    me = me_ref[0]
    for slot in range(GOT):
        routes_ref[slot] = 0
    for peer in range(peers):
        sent = jnp.int32(0)
        for edge in range(4 * TILES):
            other = adj_ref[peer, edge * 3]
            owner = lax.div(other, TILES)
            mine = (owner == me).astype(jnp.int32)
            slot = peer * SLOTS + jnp.minimum(sent, SLOTS - 1)
            strip = (other - owner * TILES) * 4 + adj_ref[peer, edge * 3 + 1]
            routes_ref[jnp.where(owner == me, slot, GOT - 1)] = jnp.where(owner == me, strip, 0)
            sent += mine
    owners = []
    for edge in range(4 * TILES):
        owners.append(lax.div(adj_ref[me, edge * 3], TILES))
        before = jnp.int32(0)
        for there in range(edge):
            before += (owners[there] == owners[edge]).astype(jnp.int32)
        routes_ref[GOT + edge] = owners[edge] * SLOTS + jnp.minimum(before, SLOTS - 1)
        routes_ref[BACK + edge] = adj_ref[me, edge * 3 + 2]
    for tile in range(TILES):
        strips[tile * 4] = field_ref[tile, 0]
        strips[tile * 4 + 1] = field_ref[tile, SIDE - 1]
        for edge, first, lane in ((2, 0, 0), (3, SIDE - 8, 7)):
            near = field_ref[tile, :, first : first + 8].astype(F32).reshape(SIDE * 8, CH)
            put(column, slice(None), near)
            strips[tile * 4 + edge] = take(column, pl.ds(lane, SIDE, stride=8)).astype(BF)
    fill(routes_ref, strips, send_ref)


def pack(me, adjacency, field):
    peers = adjacency.shape[0]
    return pl.pallas_call(
        pack_kernel,
        name="pack",
        out_shape=(struct((peers * SLOTS, SIDE, CH), BF), struct((BACK + 12,), jnp.int32)),
        in_specs=[smem(), smem(), vmem()],
        out_specs=(vmem(), smem()),
        scratch_shapes=[
            pltpu.VMEM((2, SIDE * 8, 128), F32),
            pltpu.VMEM((4 * TILES, SIDE, CH), BF),
        ],
        compiler_params=params(),
        cost_estimate=cost(0, 3_000_000),
    )(me, adjacency, field)


def pick(rows, shift_of_block, backwards):
    row = lax.broadcasted_iota(jnp.int32, (rows, SIDE), 0)
    cell = lax.broadcasted_iota(jnp.int32, (rows, SIDE), 1)
    block = row // SIDE
    place = row - block * SIDE
    source = place + shift_of_block(block)
    inside = (source >= 0) & (source < SIDE)
    if backwards is not None:
        source = jnp.where(backwards == 1, SIDE - 1 - source, source)
    return jnp.where(inside & (cell == source), 1.0, 0.0).astype(BF)


def dot(left, right):
    return jnp.dot(left, right, preferred_element_type=F32)


def dot_rows(left, right):
    return lax.dot_general(left, right, (((0,), (0,)), ((), ())), preferred_element_type=F32)


def block_of_edge(edge, k):
    return (k, 6 + k, 3 * k, 3 * k + 2)[edge]


EDGE_ROWS = (
    pl.ds(0, SIDE),
    pl.ds(CELLS - SIDE, SIDE),
    pl.ds(0, SIDE, stride=SIDE),
    pl.ds(SIDE - 1, SIDE, stride=SIDE),
)


def spread(source, out_ref, ascending):
    first = lax.broadcasted_iota(jnp.int32, (SIDE, CH), 0) == 0
    last = lax.broadcasted_iota(jnp.int32, (SIDE, CH), 0) == SIDE - 1

    def one(i, carry):
        row = source(i).astype(F32)
        earlier = jnp.where(first, 0.0, pltpu.roll(row, 1, 0)).astype(BF)
        later = jnp.where(last, 0.0, pltpu.roll(row, SIDE - 1, 0)).astype(BF)
        at = pl.ds(pl.multiple_of((i + 1) * SIDE, SIDE), SIDE)
        low, high = (earlier, later) if ascending else (later, earlier)
        out_ref[at, 0:CH] = low
        out_ref[at, CH : 2 * CH] = row.astype(BF)
        out_ref[at, 2 * CH : 3 * CH] = high
        return carry

    lax.fori_loop(0, SIDE, one, 0, unroll=4)


def clear_margin(out_ref):
    zero = jnp.zeros((SIDE, 3 * CH), BF)
    out_ref[0:SIDE, :] = zero
    out_ref[CELLS + SIDE : CELLS + 2 * SIDE, :] = zero


def conv_kernel(turned, shards, core_ref, field_ref, mine_ref, theirs_ref, *refs):
    if turned:
        part_ref, kernel_ref, turned_ref, wide = refs
    else:
        part_ref, kernel_ref, wide = refs
    depth = CH // shards
    core = core_ref[0]

    @pl.when(pl.program_id(0) == 0)
    def _():
        clear_margin(wide)
        for pair in range(shards // 2):
            for source, side in ((mine_ref, core), (theirs_ref, 1 - core)):
                base = (core_ref[1] ^ pair) * 2 * depth + side * depth
                for tap in range(9):
                    at = pl.multiple_of(tap * CH + base, depth)
                    kernel_ref[pl.ds(at, depth), :] = source[pair, 0, tap]
        if turned:
            for tap in range(9):
                turned_ref[tap * CH : (tap + 1) * CH, :] = kernel_ref[tap * CH : (tap + 1) * CH, :].T

    spread(lambda i: field_ref[0, i], wide, True)

    def chunk(c, carry):
        total = None
        for p in range(3):
            at = pl.multiple_of(c * CH + p * SIDE, SIDE)
            term = dot(wide[pl.ds(at, CH), :], kernel_ref[p * 3 * CH : (p + 1) * 3 * CH, :])
            total = term if total is None else total + term
        part_ref[pl.ds(pl.multiple_of(c * CH, CH), CH), :] = total
        return carry

    lax.fori_loop(0, CELLS // CH, chunk, 0)


def conv(core, field, mine, theirs, layer, turned):
    pieces = pl.BlockSpec((mine.shape[0], 1, *mine.shape[2:]), lambda t: (0, layer, 0, 0, 0))
    shards = mine.shape[0] * 2
    outs = [struct((TILES * CELLS, CH), F32), struct((9 * CH, CH), BF)]
    specs = [per_tile(CELLS, CH), whole((9 * CH, CH))]
    if turned:
        outs.append(struct((9 * CH, CH), BF))
        specs.append(whole((9 * CH, CH)))
    return pl.pallas_call(
        lambda *refs: conv_kernel(turned, shards, *refs),
        name="conv_turned" if turned else "conv",
        out_shape=tuple(outs),
        grid=(TILES,),
        in_specs=[smem(), per_tile(1, SIDE, SIDE, CH), pieces, pieces],
        out_specs=tuple(specs),
        scratch_shapes=[pltpu.VMEM((CELLS + 2 * SIDE, 3 * CH), BF)],
        compiler_params=params(1),
        cost_estimate=cost(3_600_000_000, 7_000_000),
    )(core, field, mine, theirs)


def add_rims(routes_ref, got_ref, kernel_ref, rows3, rim_part):
    for edge in range(4):
        for tile in range(TILES):
            back = routes_ref[BACK + tile * 4 + edge]
            choose = pick(3 * SIDE, lambda block: block - 1, back)
            shifted = dot(choose, got_ref[routes_ref[GOT + tile * 4 + edge]]).astype(BF)
            for k in range(3):
                rows3[tile * SIDE : (tile + 1) * SIDE, k * CH : (k + 1) * CH] = shifted[
                    k * SIDE : (k + 1) * SIDE
                ]
        total = None
        for k in range(3):
            block = block_of_edge(edge, k)
            term = dot(
                rows3[:, k * CH : (k + 1) * CH], kernel_ref[block * CH : (block + 1) * CH, :]
            )
            total = term if total is None else total + term
        rim_part[edge] = total


def with_rims(part_ref, rim_part, out):
    tile = pl.program_id(0)
    put(out, slice(None), part_ref[...])
    for edge in range(4):
        rows = EDGE_ROWS[edge]
        add = rim_part[edge, pl.ds(pl.multiple_of(tile * SIDE, SIDE), SIDE), :]
        put(out, rows, take(out, rows) + add)


def finish_kernel(
    routes_ref,
    part_ref,
    field_ref,
    got_ref,
    kernel_ref,
    state_ref,
    slope_ref,
    send_ref,
    rows3,
    rim_part,
    fresh,
    strips,
):
    tile = pl.program_id(0)

    @pl.when(tile == 0)
    def _():
        add_rims(routes_ref, got_ref, kernel_ref, rows3, rim_part)

    with_rims(part_ref, rim_part, fresh)

    def one(i, carry):
        at = pl.ds(pl.multiple_of(i * SIDE, SIDE), SIDE)
        v = take(fresh, at)
        s = 1.0 / (1.0 + jnp.exp(-v))
        updated = field_ref[0, i].astype(F32) + v * s
        put(fresh, at, updated)
        state_ref[0, i] = updated.astype(BF)
        slope_ref[at, :] = s * (1.0 + v * (1.0 - s))
        return carry

    lax.fori_loop(0, SIDE, one, 0, unroll=4)
    for edge in range(4):
        strips[tile * 4 + edge] = take(fresh, EDGE_ROWS[edge]).astype(BF)

    @pl.when(tile == TILES - 1)
    def _():
        fill(routes_ref, strips, send_ref)


def finish(routes, part, field, got, kernel):
    return pl.pallas_call(
        finish_kernel,
        name="finish",
        out_shape=(
            struct(field.shape, BF),
            struct(part.shape, F32),
            struct(got.shape, BF),
        ),
        grid=(TILES,),
        in_specs=[
            smem(),
            per_tile(CELLS, CH),
            per_tile(1, SIDE, SIDE, CH),
            whole(got.shape),
            whole(kernel.shape),
        ],
        out_specs=(per_tile(1, SIDE, SIDE, CH), per_tile(CELLS, CH), whole(got.shape)),
        scratch_shapes=[
            pltpu.VMEM((TILES * SIDE, 3 * CH), BF),
            pltpu.VMEM((4, TILES * SIDE, CH), F32),
            pltpu.VMEM((2, CELLS, 128), F32),
            pltpu.VMEM((4 * TILES, SIDE, CH), BF),
        ],
        compiler_params=params(1),
        cost_estimate=cost(200_000_000, 10_000_000),
    )(routes, part, field, got, kernel)


def note_strips(grad, triples, tile):
    choose = pick(3 * SIDE, lambda block: 1 - block, None)
    for edge in range(4):
        shifted = dot(choose, take(grad, EDGE_ROWS[edge]).astype(BF)).astype(BF)
        for k in range(3):
            triples[
                edge, pl.ds(pl.multiple_of(tile * SIDE, SIDE), SIDE), k * CH : (k + 1) * CH
            ] = shifted[k * SIDE : (k + 1) * SIDE]


def last_kernel(
    routes_ref,
    part_ref,
    field_ref,
    got_ref,
    kernel_ref,
    turned_ref,
    cot_ref,
    state_ref,
    grad_ref,
    send_ref,
    triples_ref,
    rows3,
    rim_part,
    fresh,
    strips,
):
    tile = pl.program_id(0)

    @pl.when(tile == 0)
    def _():
        add_rims(routes_ref, got_ref, kernel_ref, rows3, rim_part)

    with_rims(part_ref, rim_part, fresh)

    def one(i, carry):
        at = pl.ds(pl.multiple_of(i * SIDE, SIDE), SIDE)
        v = take(fresh, at)
        s = 1.0 / (1.0 + jnp.exp(-v))
        state_ref[0, i] = (field_ref[0, i].astype(F32) + v * s).astype(BF)
        grad = cot_ref[0, i].astype(F32) * s * (1.0 + v * (1.0 - s))
        put(fresh, at, grad)
        grad_ref[at, :] = grad.astype(BF)
        return carry

    lax.fori_loop(0, SIDE, one, 0, unroll=4)
    note_strips(fresh, triples_ref, tile)

    @pl.when(tile == TILES - 1)
    def _():
        for edge in range(4):
            total = None
            for k in range(3):
                block = block_of_edge(edge, k)
                term = dot(
                    triples_ref[edge, :, k * CH : (k + 1) * CH],
                    turned_ref[block * CH : (block + 1) * CH, :],
                )
                total = term if total is None else total + term
            for there in range(TILES):
                strips[there * 4 + edge] = total[there * SIDE : (there + 1) * SIDE].astype(BF)
        fill(routes_ref, strips, send_ref)


def last(routes, part, field, got, kernel, turned, cotangent):
    triples = (4, TILES * SIDE, 3 * CH)
    return pl.pallas_call(
        last_kernel,
        name="last",
        out_shape=(
            struct(field.shape, BF),
            struct((TILES * CELLS, CH), BF),
            struct(got.shape, BF),
            struct(triples, BF),
        ),
        grid=(TILES,),
        in_specs=[
            smem(),
            per_tile(CELLS, CH),
            per_tile(1, SIDE, SIDE, CH),
            whole(got.shape),
            whole(kernel.shape),
            whole(turned.shape),
            per_tile(1, SIDE, SIDE, CH),
        ],
        out_specs=(
            per_tile(1, SIDE, SIDE, CH),
            per_tile(CELLS, CH),
            whole(got.shape),
            whole(triples),
        ),
        scratch_shapes=[
            pltpu.VMEM((TILES * SIDE, 3 * CH), BF),
            pltpu.VMEM((4, TILES * SIDE, CH), F32),
            pltpu.VMEM((2, CELLS, 128), F32),
            pltpu.VMEM((4 * TILES, SIDE, CH), BF),
        ],
        compiler_params=params(1),
        cost_estimate=cost(400_000_000, 12_000_000),
    )(routes, part, field, got, kernel, turned, cotangent)


def outer(field, wide, across, total):
    across[...] = field.reshape(CELLS, CH).T

    def one(p, carry):
        at = pl.multiple_of((2 - p) * SIDE, SIDE)
        total[p] = total[p] + dot(across[...], wide[pl.ds(at, CELLS), :])
        return carry

    lax.fori_loop(0, 3, one, 0)


def outer_rims(routes_ref, got_ref, triples, total, flat):
    for edge in range(4):
        for tile in range(TILES):
            back = routes_ref[BACK + tile * 4 + edge]
            choose = pick(SIDE, lambda block: 0, back)
            flat[tile * SIDE : (tile + 1) * SIDE, :] = dot(
                choose, got_ref[routes_ref[GOT + tile * 4 + edge]]
            ).astype(BF)
        for k in range(3):
            p, q = divmod(block_of_edge(edge, k), 3)
            lanes = slice(q * CH, (q + 1) * CH)
            total[p, :, lanes] = total[p, :, lanes] + dot_rows(
                flat[...], triples[edge, :, k * CH : (k + 1) * CH]
            )


def hand_over(core, total, kept_ref, given_ref):
    pairs = kept_ref.shape[0]
    depth = kept_ref.shape[2]
    for pair in range(pairs):
        own = pl.ds(pl.multiple_of(pair * 2 * depth + core * depth, depth), depth)
        other = pl.ds(pl.multiple_of(pair * 2 * depth + (1 - core) * depth, depth), depth)
        for tap in range(9):
            p, q = divmod(tap, 3)
            kept_ref[pair, tap] = total[p, own, q * CH : (q + 1) * CH]
            given_ref[pair, tap] = total[p, other, q * CH : (q + 1) * CH].astype(BF)


def second_kernel(
    routes_ref,
    core_ref,
    field_ref,
    grad_ref,
    got_ref,
    triples_ref,
    turned_ref,
    back_ref,
    kept_ref,
    given_ref,
    wide,
    across,
    total,
    flat,
):
    tile = pl.program_id(0)

    @pl.when(tile == 0)
    def _():
        clear_margin(wide)
        total[...] = jnp.zeros_like(total)

    spread(lambda i: grad_ref[pl.ds(pl.multiple_of(i * SIDE, SIDE), SIDE), :], wide, False)

    def chunk(c, carry):
        result = None
        for p in range(3):
            at = pl.multiple_of(c * CH + (2 - p) * SIDE, SIDE)
            term = dot(wide[pl.ds(at, CH), :], turned_ref[p * 3 * CH : (p + 1) * 3 * CH, :])
            result = term if result is None else result + term
        back_ref[pl.ds(pl.multiple_of(c * CH, CH), CH), :] = result
        return carry

    lax.fori_loop(0, CELLS // CH, chunk, 0)
    outer(field_ref[0], wide, across, total)

    @pl.when(tile == TILES - 1)
    def _():
        outer_rims(routes_ref, got_ref, triples_ref, total, flat)
        hand_over(core_ref[0], total, kept_ref, given_ref)


def second(routes, core, field, grad, got, triples, turned, pairs, depth):
    half = (pairs, 9, depth, CH)
    return pl.pallas_call(
        second_kernel,
        name="second",
        out_shape=(struct((TILES * CELLS, CH), F32), struct(half, F32), struct(half, BF)),
        grid=(TILES,),
        in_specs=[
            smem(),
            smem(),
            per_tile(1, SIDE, SIDE, CH),
            per_tile(CELLS, CH),
            whole(got.shape),
            whole(triples.shape),
            whole(turned.shape),
        ],
        out_specs=(per_tile(CELLS, CH), whole(half), whole(half)),
        scratch_shapes=[
            pltpu.VMEM((CELLS + 2 * SIDE, 3 * CH), BF),
            pltpu.VMEM((CH, CELLS), BF),
            pltpu.VMEM((3, CH, 3 * CH), F32),
            pltpu.VMEM((TILES * SIDE, CH), BF),
        ],
        compiler_params=params(1),
        cost_estimate=cost(7_200_000_000, 12_000_000),
    )(routes, core, field, grad, got, triples, turned)


def first_kernel(
    routes_ref,
    core_ref,
    field_ref,
    cot_ref,
    back_ref,
    slope_ref,
    got_ref,
    returned_ref,
    kept_ref,
    given_ref,
    wide,
    across,
    total,
    flat,
    fresh,
    triples,
):
    tile = pl.program_id(0)

    @pl.when(tile == 0)
    def _():
        clear_margin(wide)
        total[...] = jnp.zeros_like(total)

    def one(i, carry):
        at = pl.ds(pl.multiple_of(i * SIDE, SIDE), SIDE)
        put(fresh, at, cot_ref[0, i].astype(F32) + back_ref[at, :])
        return carry

    lax.fori_loop(0, SIDE, one, 0, unroll=4)
    for edge in range(4):
        back = routes_ref[BACK + tile * 4 + edge]
        choose = pick(SIDE, lambda block: 0, back)
        rows = EDGE_ROWS[edge]
        add = dot(choose, returned_ref[routes_ref[GOT + tile * 4 + edge]])
        put(fresh, rows, take(fresh, rows) + add)

    def two(i, carry):
        at = pl.ds(pl.multiple_of(i * SIDE, SIDE), SIDE)
        put(fresh, at, take(fresh, at) * slope_ref[at, :])
        return carry

    lax.fori_loop(0, SIDE, two, 0, unroll=4)
    note_strips(fresh, triples, tile)
    spread(lambda i: take(fresh, pl.ds(pl.multiple_of(i * SIDE, SIDE), SIDE)), wide, False)
    outer(field_ref[0], wide, across, total)

    @pl.when(tile == TILES - 1)
    def _():
        outer_rims(routes_ref, got_ref, triples, total, flat)
        hand_over(core_ref[0], total, kept_ref, given_ref)


def first(routes, core, field, cotangent, back, slope, got, returned, pairs, depth):
    half = (pairs, 9, depth, CH)
    return pl.pallas_call(
        first_kernel,
        name="first",
        out_shape=(struct(half, F32), struct(half, BF)),
        grid=(TILES,),
        in_specs=[
            smem(),
            smem(),
            per_tile(1, SIDE, SIDE, CH),
            per_tile(1, SIDE, SIDE, CH),
            per_tile(CELLS, CH),
            per_tile(CELLS, CH),
            whole(got.shape),
            whole(returned.shape),
        ],
        out_specs=(whole(half), whole(half)),
        scratch_shapes=[
            pltpu.VMEM((CELLS + 2 * SIDE, 3 * CH), BF),
            pltpu.VMEM((CH, CELLS), BF),
            pltpu.VMEM((3, CH, 3 * CH), F32),
            pltpu.VMEM((TILES * SIDE, CH), BF),
            pltpu.VMEM((2, CELLS, 128), F32),
            pltpu.VMEM((4, TILES * SIDE, 3 * CH), BF),
        ],
        compiler_params=params(1),
        cost_estimate=cost(3_600_000_000, 12_000_000),
    )(routes, core, field, cotangent, back, slope, got, returned)


def cut_kernel(kept1_ref, got1_ref, kept2_ref, got2_ref, out_ref, rows):
    depth = kept1_ref.shape[2]
    run = 9 * depth // 4
    for layer, (kept_ref, got_ref) in enumerate(((kept1_ref, got1_ref), (kept2_ref, got2_ref))):
        for tap in range(9):
            rows[layer, tap * depth : (tap + 1) * depth, :] = kept_ref[0, tap] + got_ref[
                0, tap
            ].astype(F32)
        for peer in range(8):
            high, low = divmod(peer, 4)
            out_ref[peer, layer * run : (layer + 1) * run, :] = rows[
                layer, low * run : (low + 1) * run, high * 128 : (high + 1) * 128
            ].astype(BF)


def cut(kept1, got1, kept2, got2):
    pairs, _, depth, _ = kept1.shape
    run = 9 * depth // 4
    return pl.pallas_call(
        cut_kernel,
        name="cut",
        out_shape=struct((pairs * 8, 2 * run, 128), BF),
        grid=(pairs,),
        in_specs=[per_tile(1, 9, depth, CH)] * 4,
        out_specs=per_tile(8, 2 * run, 128),
        scratch_shapes=[pltpu.VMEM((2, 9 * depth, CH), F32)],
        compiler_params=params(1),
        cost_estimate=cost(0, 6_000_000),
    )(kept1, got1, kept2, got2)


def sum_kernel(in_ref, out_ref):
    summed = in_ref[0].astype(F32)
    for other in range(1, in_ref.shape[0]):
        summed = summed + in_ref[other].astype(F32)
    for peer in range(out_ref.shape[0]):
        out_ref[peer] = summed


def sum_all(parts, peers):
    return pl.pallas_call(
        sum_kernel,
        name="sum_all",
        out_shape=struct((peers, *parts.shape[1:]), F32),
        in_specs=[vmem()],
        out_specs=vmem(),
        compiler_params=params(),
        cost_estimate=cost(0, 2_000_000),
    )(parts)


def join_kernel(in_ref, out_ref):
    peers = in_ref.shape[0]
    run = in_ref.shape[1] // 2
    rows_all = out_ref.shape[0] // 2
    for layer in range(2):
        for peer in range(peers):
            high, low = divmod(peer, 4)
            at = layer * rows_all + low * run
            out_ref[at : at + run, high * 128 : (high + 1) * 128] = in_ref[
                peer, layer * run : (layer + 1) * run
            ]


def join(blocks, depth):
    return pl.pallas_call(
        join_kernel,
        name="join",
        out_shape=struct((2 * 9 * depth, CH), F32),
        in_specs=[vmem()],
        out_specs=vmem(),
        compiler_params=params(),
        cost_estimate=cost(0, 600_000),
    )(blocks)


def exchange(value, axes, groups=None):
    return lax.all_to_all(value, axes, 0, 0, tiled=True, axis_index_groups=groups)


def solution(mesh):
    shards, peers = mesh.shape["dp"], mesh.shape["space"]
    pairs, depth = shards // 2, CH // shards
    same_core_all = [
        [(pair * 2 + core) * peers + peer for pair in range(pairs) for peer in range(peers)]
        for core in range(2)
    ]
    swap = [(index, index ^ 1) for index in range(shards)]

    def gather(shard):
        blocks = []
        for step in range(1, pairs):
            route = [(index, index ^ (2 * step)) for index in range(shards)]
            blocks.append(lax.ppermute(shard, "dp", route))
        return blocks

    def trade(strips):
        return exchange(strips.reshape(peers, SLOTS, SIDE, CH), "space").reshape(strips.shape)

    def per_device(inputs, kernels, cotangent, adjacency):
        place = lax.axis_index("dp").astype(jnp.int32)
        core = jnp.stack([place % 2, place // 2])
        me = lax.axis_index("space").astype(jnp.int32).reshape(1)
        edges = exchange(jnp.broadcast_to(adjacency.reshape(1, 36), (peers, 36)), "space")
        blocks = gather(kernels.reshape(2, 9, depth, CH))
        field = inputs[0]
        cot = cotangent[0]
        send1, routes = pack(me, edges, field)
        own, send1 = lax.optimization_barrier((kernels.reshape(2, 9, depth, CH), send1))
        got1 = trade(send1)
        mine = jnp.stack([own, *blocks])
        theirs = lax.ppermute(mine, "dp", swap)
        part1, kernel1 = conv(core, field, mine, theirs, 0, False)
        state1, slope1, send2 = finish(routes, part1, field, got1, kernel1)
        got2 = trade(send2)
        part2, kernel2, turned2 = conv(core, state1, mine, theirs, 1, True)
        state2, grad2, send3, triples2 = last(routes, part2, state1, got2, kernel2, turned2, cot)
        returned = trade(send3)
        back, kept2, given2 = second(
            routes, core, state1, grad2, got2, triples2, turned2, pairs, depth
        )
        got_half2 = lax.ppermute(given2, "dp", swap)
        kept1, given1 = first(
            routes, core, field, cot, back, slope1, got1, returned, pairs, depth
        )
        blocks = cut(kept1, lax.ppermute(given1, "dp", swap), kept2, got_half2)
        summed = sum_all(exchange(blocks, ("dp", "space"), same_core_all), peers)
        grads = join(exchange(summed, "space"), depth)
        return state2[None], grads.reshape(2, 3, 3, depth, CH)

    in_specs = (
        P("dp", "space", None, None, None),
        P(None, None, None, "dp", None),
        P("dp", "space", None, None, None),
        P("space", None, None),
    )
    out_specs = (P("dp", "space", None, None, None), P(None, None, None, "dp", None))
    return jax.shard_map(
        per_device, mesh=mesh, in_specs=in_specs, out_specs=out_specs, check_vma=False
    )
```

```python
import jax
import jax.numpy as jnp
from jax import lax
from jax.experimental import pallas as pl
from jax.experimental.pallas import tpu as pltpu
from jax.sharding import PartitionSpec as P

BF = jnp.bfloat16
F32 = jnp.float32
TILES, SIDE, CH = 3, 32, 256
CELLS = SIDE * SIDE
SLOTS = 7
GOT, BACK = 64, 76


def vmem():
    return pl.BlockSpec(memory_space=pltpu.VMEM)


def smem():
    return pl.BlockSpec(memory_space=pltpu.SMEM)


def whole(shape):
    zeros = (0,) * len(shape)
    return pl.BlockSpec(shape, lambda t: zeros)


def per_tile(*tail):
    zeros = (0,) * (len(tail) - 1)
    return pl.BlockSpec(tail, lambda t: (t, *zeros))


def struct(shape, dtype):
    return jax.ShapeDtypeStruct(shape, dtype)


def params(steps=0):
    if steps:
        return pltpu.CompilerParams(
            dimension_semantics=("arbitrary",), vmem_limit_bytes=60 * 1024 * 1024
        )
    return pltpu.CompilerParams(vmem_limit_bytes=60 * 1024 * 1024)


def cost(flops, moved):
    return pl.CostEstimate(flops=flops, bytes_accessed=moved, transcendentals=0)


def take(halves, rows):
    return jnp.concatenate([halves[0, rows, :], halves[1, rows, :]], axis=1)


def put(halves, rows, value):
    halves[0, rows, :] = value[:, 0:128]
    halves[1, rows, :] = value[:, 128:256]


def fill(routes_ref, strips, send_ref):
    for slot in range(send_ref.shape[0]):
        send_ref[slot] = strips[routes_ref[slot]]


def pack_kernel(me_ref, adj_ref, field_ref, send_ref, routes_ref, column, strips):
    peers = adj_ref.shape[0]
    me = me_ref[0]
    for slot in range(GOT):
        routes_ref[slot] = 0
    for peer in range(peers):
        sent = jnp.int32(0)
        for edge in range(4 * TILES):
            other = adj_ref[peer, edge * 3]
            owner = lax.div(other, TILES)
            mine = (owner == me).astype(jnp.int32)
            slot = peer * SLOTS + jnp.minimum(sent, SLOTS - 1)
            strip = (other - owner * TILES) * 4 + adj_ref[peer, edge * 3 + 1]
            routes_ref[jnp.where(owner == me, slot, GOT - 1)] = jnp.where(owner == me, strip, 0)
            sent += mine
    owners = []
    for edge in range(4 * TILES):
        owners.append(lax.div(adj_ref[me, edge * 3], TILES))
        before = jnp.int32(0)
        for there in range(edge):
            before += (owners[there] == owners[edge]).astype(jnp.int32)
        routes_ref[GOT + edge] = owners[edge] * SLOTS + jnp.minimum(before, SLOTS - 1)
        routes_ref[BACK + edge] = adj_ref[me, edge * 3 + 2]
    for tile in range(TILES):
        strips[tile * 4] = field_ref[tile, 0]
        strips[tile * 4 + 1] = field_ref[tile, SIDE - 1]
        for edge, first, lane in ((2, 0, 0), (3, SIDE - 8, 7)):
            near = field_ref[tile, :, first : first + 8].astype(F32).reshape(SIDE * 8, CH)
            put(column, slice(None), near)
            strips[tile * 4 + edge] = take(column, pl.ds(lane, SIDE, stride=8)).astype(BF)
    fill(routes_ref, strips, send_ref)


def pack(me, adjacency, field):
    peers = adjacency.shape[0]
    return pl.pallas_call(
        pack_kernel,
        name="pack",
        out_shape=(struct((peers * SLOTS, SIDE, CH), BF), struct((BACK + 12,), jnp.int32)),
        in_specs=[smem(), smem(), vmem()],
        out_specs=(vmem(), smem()),
        scratch_shapes=[
            pltpu.VMEM((2, SIDE * 8, 128), F32),
            pltpu.VMEM((4 * TILES, SIDE, CH), BF),
        ],
        compiler_params=params(),
        cost_estimate=cost(0, 3_000_000),
    )(me, adjacency, field)


def pick(rows, shift_of_block, backwards):
    row = lax.broadcasted_iota(jnp.int32, (rows, SIDE), 0)
    cell = lax.broadcasted_iota(jnp.int32, (rows, SIDE), 1)
    block = row // SIDE
    place = row - block * SIDE
    source = place + shift_of_block(block)
    inside = (source >= 0) & (source < SIDE)
    if backwards is not None:
        source = jnp.where(backwards == 1, SIDE - 1 - source, source)
    return jnp.where(inside & (cell == source), 1.0, 0.0).astype(BF)


def dot(left, right):
    return jnp.dot(left, right, preferred_element_type=F32)


def dot_rows(left, right):
    return lax.dot_general(left, right, (((0,), (0,)), ((), ())), preferred_element_type=F32)


def block_of_edge(edge, k):
    return (k, 6 + k, 3 * k, 3 * k + 2)[edge]


EDGE_ROWS = (
    pl.ds(0, SIDE),
    pl.ds(CELLS - SIDE, SIDE),
    pl.ds(0, SIDE, stride=SIDE),
    pl.ds(SIDE - 1, SIDE, stride=SIDE),
)


def spread(source, out_ref, ascending):
    first = lax.broadcasted_iota(jnp.int32, (SIDE, CH), 0) == 0
    last = lax.broadcasted_iota(jnp.int32, (SIDE, CH), 0) == SIDE - 1

    def one(i, carry):
        row = source(i).astype(F32)
        earlier = jnp.where(first, 0.0, pltpu.roll(row, 1, 0)).astype(BF)
        later = jnp.where(last, 0.0, pltpu.roll(row, SIDE - 1, 0)).astype(BF)
        at = pl.ds(pl.multiple_of((i + 1) * SIDE, SIDE), SIDE)
        low, high = (earlier, later) if ascending else (later, earlier)
        out_ref[at, 0:CH] = low
        out_ref[at, CH : 2 * CH] = row.astype(BF)
        out_ref[at, 2 * CH : 3 * CH] = high
        return carry

    lax.fori_loop(0, SIDE, one, 0, unroll=4)


def clear_margin(out_ref):
    zero = jnp.zeros((SIDE, 3 * CH), BF)
    out_ref[0:SIDE, :] = zero
    out_ref[CELLS + SIDE : CELLS + 2 * SIDE, :] = zero


def conv_kernel(turned, shards, core_ref, field_ref, mine_ref, theirs_ref, *refs):
    if turned:
        part_ref, kernel_ref, turned_ref, wide = refs
    else:
        part_ref, kernel_ref, wide = refs
    depth = CH // shards
    core = core_ref[0]

    @pl.when(pl.program_id(0) == 0)
    def _():
        clear_margin(wide)
        for pair in range(shards // 2):
            for source, side in ((mine_ref, core), (theirs_ref, 1 - core)):
                base = (core_ref[1] ^ pair) * 2 * depth + side * depth
                for tap in range(9):
                    at = pl.multiple_of(tap * CH + base, depth)
                    kernel_ref[pl.ds(at, depth), :] = source[pair, 0, tap]
        if turned:
            for tap in range(9):
                turned_ref[tap * CH : (tap + 1) * CH, :] = kernel_ref[tap * CH : (tap + 1) * CH, :].T

    spread(lambda i: field_ref[0, i], wide, True)

    def chunk(c, carry):
        total = None
        for p in range(3):
            at = pl.multiple_of(c * CH + p * SIDE, SIDE)
            term = dot(wide[pl.ds(at, CH), :], kernel_ref[p * 3 * CH : (p + 1) * 3 * CH, :])
            total = term if total is None else total + term
        part_ref[pl.ds(pl.multiple_of(c * CH, CH), CH), :] = total.astype(BF)
        return carry

    lax.fori_loop(0, CELLS // CH, chunk, 0)


def conv(core, field, mine, theirs, layer, turned):
    pieces = pl.BlockSpec((mine.shape[0], 1, *mine.shape[2:]), lambda t: (0, layer, 0, 0, 0))
    shards = mine.shape[0] * 2
    outs = [struct((TILES * CELLS, CH), BF), struct((9 * CH, CH), BF)]
    specs = [per_tile(CELLS, CH), whole((9 * CH, CH))]
    if turned:
        outs.append(struct((9 * CH, CH), BF))
        specs.append(whole((9 * CH, CH)))
    return pl.pallas_call(
        lambda *refs: conv_kernel(turned, shards, *refs),
        name="conv_turned" if turned else "conv",
        out_shape=tuple(outs),
        grid=(TILES,),
        in_specs=[smem(), per_tile(1, SIDE, SIDE, CH), pieces, pieces],
        out_specs=tuple(specs),
        scratch_shapes=[pltpu.VMEM((CELLS + 2 * SIDE, 3 * CH), BF)],
        compiler_params=params(1),
        cost_estimate=cost(3_600_000_000, 7_000_000),
    )(core, field, mine, theirs)


def add_rims(routes_ref, got_ref, kernel_ref, rows3, rim_part):
    for edge in range(4):
        for tile in range(TILES):
            back = routes_ref[BACK + tile * 4 + edge]
            choose = pick(3 * SIDE, lambda block: block - 1, back)
            shifted = dot(choose, got_ref[routes_ref[GOT + tile * 4 + edge]]).astype(BF)
            for k in range(3):
                rows3[tile * SIDE : (tile + 1) * SIDE, k * CH : (k + 1) * CH] = shifted[
                    k * SIDE : (k + 1) * SIDE
                ]
        total = None
        for k in range(3):
            block = block_of_edge(edge, k)
            term = dot(
                rows3[:, k * CH : (k + 1) * CH], kernel_ref[block * CH : (block + 1) * CH, :]
            )
            total = term if total is None else total + term
        rim_part[edge] = total


def with_rims(part_ref, rim_part, out):
    tile = pl.program_id(0)
    put(out, slice(None), part_ref[...].astype(F32))
    for edge in range(4):
        rows = EDGE_ROWS[edge]
        add = rim_part[edge, pl.ds(pl.multiple_of(tile * SIDE, SIDE), SIDE), :]
        put(out, rows, take(out, rows) + add)


def finish_kernel(
    routes_ref,
    part_ref,
    field_ref,
    got_ref,
    kernel_ref,
    state_ref,
    slope_ref,
    send_ref,
    rows3,
    rim_part,
    fresh,
    strips,
):
    tile = pl.program_id(0)

    @pl.when(tile == 0)
    def _():
        add_rims(routes_ref, got_ref, kernel_ref, rows3, rim_part)

    with_rims(part_ref, rim_part, fresh)

    def one(i, carry):
        at = pl.ds(pl.multiple_of(i * SIDE, SIDE), SIDE)
        v = take(fresh, at)
        s = 1.0 / (1.0 + jnp.exp(-v))
        updated = field_ref[0, i].astype(F32) + v * s
        put(fresh, at, updated)
        state_ref[0, i] = updated.astype(BF)
        slope_ref[at, :] = (s * (1.0 + v * (1.0 - s))).astype(BF)
        return carry

    lax.fori_loop(0, SIDE, one, 0, unroll=4)
    for edge in range(4):
        strips[tile * 4 + edge] = take(fresh, EDGE_ROWS[edge]).astype(BF)

    @pl.when(tile == TILES - 1)
    def _():
        fill(routes_ref, strips, send_ref)


def finish(routes, part, field, got, kernel):
    return pl.pallas_call(
        finish_kernel,
        name="finish",
        out_shape=(
            struct(field.shape, BF),
            struct(part.shape, BF),
            struct(got.shape, BF),
        ),
        grid=(TILES,),
        in_specs=[
            smem(),
            per_tile(CELLS, CH),
            per_tile(1, SIDE, SIDE, CH),
            whole(got.shape),
            whole(kernel.shape),
        ],
        out_specs=(per_tile(1, SIDE, SIDE, CH), per_tile(CELLS, CH), whole(got.shape)),
        scratch_shapes=[
            pltpu.VMEM((TILES * SIDE, 3 * CH), BF),
            pltpu.VMEM((4, TILES * SIDE, CH), F32),
            pltpu.VMEM((2, CELLS, 128), F32),
            pltpu.VMEM((4 * TILES, SIDE, CH), BF),
        ],
        compiler_params=params(1),
        cost_estimate=cost(200_000_000, 10_000_000),
    )(routes, part, field, got, kernel)


def note_strips(grad, triples, tile):
    choose = pick(3 * SIDE, lambda block: 1 - block, None)
    for edge in range(4):
        shifted = dot(choose, take(grad, EDGE_ROWS[edge]).astype(BF)).astype(BF)
        for k in range(3):
            triples[
                edge, pl.ds(pl.multiple_of(tile * SIDE, SIDE), SIDE), k * CH : (k + 1) * CH
            ] = shifted[k * SIDE : (k + 1) * SIDE]


def last_kernel(
    routes_ref,
    part_ref,
    field_ref,
    got_ref,
    kernel_ref,
    turned_ref,
    cot_ref,
    state_ref,
    grad_ref,
    send_ref,
    triples_ref,
    rows3,
    rim_part,
    fresh,
    strips,
):
    tile = pl.program_id(0)

    @pl.when(tile == 0)
    def _():
        add_rims(routes_ref, got_ref, kernel_ref, rows3, rim_part)

    with_rims(part_ref, rim_part, fresh)

    def one(i, carry):
        at = pl.ds(pl.multiple_of(i * SIDE, SIDE), SIDE)
        v = take(fresh, at)
        s = 1.0 / (1.0 + jnp.exp(-v))
        state_ref[0, i] = (field_ref[0, i].astype(F32) + v * s).astype(BF)
        grad = cot_ref[0, i].astype(F32) * s * (1.0 + v * (1.0 - s))
        put(fresh, at, grad)
        grad_ref[at, :] = grad.astype(BF)
        return carry

    lax.fori_loop(0, SIDE, one, 0, unroll=4)
    note_strips(fresh, triples_ref, tile)

    @pl.when(tile == TILES - 1)
    def _():
        for edge in range(4):
            total = None
            for k in range(3):
                block = block_of_edge(edge, k)
                term = dot(
                    triples_ref[edge, :, k * CH : (k + 1) * CH],
                    turned_ref[block * CH : (block + 1) * CH, :],
                )
                total = term if total is None else total + term
            for there in range(TILES):
                strips[there * 4 + edge] = total[there * SIDE : (there + 1) * SIDE].astype(BF)
        fill(routes_ref, strips, send_ref)


def last(routes, part, field, got, kernel, turned, cotangent):
    triples = (4, TILES * SIDE, 3 * CH)
    return pl.pallas_call(
        last_kernel,
        name="last",
        out_shape=(
            struct(field.shape, BF),
            struct((TILES * CELLS, CH), BF),
            struct(got.shape, BF),
            struct(triples, BF),
        ),
        grid=(TILES,),
        in_specs=[
            smem(),
            per_tile(CELLS, CH),
            per_tile(1, SIDE, SIDE, CH),
            whole(got.shape),
            whole(kernel.shape),
            whole(turned.shape),
            per_tile(1, SIDE, SIDE, CH),
        ],
        out_specs=(
            per_tile(1, SIDE, SIDE, CH),
            per_tile(CELLS, CH),
            whole(got.shape),
            whole(triples),
        ),
        scratch_shapes=[
            pltpu.VMEM((TILES * SIDE, 3 * CH), BF),
            pltpu.VMEM((4, TILES * SIDE, CH), F32),
            pltpu.VMEM((2, CELLS, 128), F32),
            pltpu.VMEM((4 * TILES, SIDE, CH), BF),
        ],
        compiler_params=params(1),
        cost_estimate=cost(400_000_000, 12_000_000),
    )(routes, part, field, got, kernel, turned, cotangent)


def outer(field, wide, across, total):
    across[...] = field.reshape(CELLS, CH).T

    def one(p, carry):
        at = pl.multiple_of((2 - p) * SIDE, SIDE)
        total[p] = total[p] + dot(across[...], wide[pl.ds(at, CELLS), :])
        return carry

    lax.fori_loop(0, 3, one, 0)


def outer_rims(routes_ref, got_ref, triples, total, flat):
    for edge in range(4):
        for tile in range(TILES):
            back = routes_ref[BACK + tile * 4 + edge]
            choose = pick(SIDE, lambda block: 0, back)
            flat[tile * SIDE : (tile + 1) * SIDE, :] = dot(
                choose, got_ref[routes_ref[GOT + tile * 4 + edge]]
            ).astype(BF)
        for k in range(3):
            p, q = divmod(block_of_edge(edge, k), 3)
            lanes = slice(q * CH, (q + 1) * CH)
            total[p, :, lanes] = total[p, :, lanes] + dot_rows(
                flat[...], triples[edge, :, k * CH : (k + 1) * CH]
            )


def hand_over(core, total, kept_ref, given_ref):
    pairs = kept_ref.shape[0]
    depth = kept_ref.shape[2]
    for pair in range(pairs):
        own = pl.ds(pl.multiple_of(pair * 2 * depth + core * depth, depth), depth)
        other = pl.ds(pl.multiple_of(pair * 2 * depth + (1 - core) * depth, depth), depth)
        for tap in range(9):
            p, q = divmod(tap, 3)
            kept_ref[pair, tap] = total[p, own, q * CH : (q + 1) * CH]
            given_ref[pair, tap] = total[p, other, q * CH : (q + 1) * CH].astype(BF)


def second_kernel(
    routes_ref,
    core_ref,
    field_ref,
    grad_ref,
    got_ref,
    triples_ref,
    turned_ref,
    back_ref,
    kept_ref,
    given_ref,
    wide,
    across,
    total,
    flat,
):
    tile = pl.program_id(0)

    @pl.when(tile == 0)
    def _():
        clear_margin(wide)
        total[...] = jnp.zeros_like(total)

    spread(lambda i: grad_ref[pl.ds(pl.multiple_of(i * SIDE, SIDE), SIDE), :], wide, False)

    def chunk(c, carry):
        result = None
        for p in range(3):
            at = pl.multiple_of(c * CH + (2 - p) * SIDE, SIDE)
            term = dot(wide[pl.ds(at, CH), :], turned_ref[p * 3 * CH : (p + 1) * 3 * CH, :])
            result = term if result is None else result + term
        back_ref[pl.ds(pl.multiple_of(c * CH, CH), CH), :] = result
        return carry

    lax.fori_loop(0, CELLS // CH, chunk, 0)
    outer(field_ref[0], wide, across, total)

    @pl.when(tile == TILES - 1)
    def _():
        outer_rims(routes_ref, got_ref, triples_ref, total, flat)
        hand_over(core_ref[0], total, kept_ref, given_ref)


def second(routes, core, field, grad, got, triples, turned, pairs, depth):
    half = (pairs, 9, depth, CH)
    return pl.pallas_call(
        second_kernel,
        name="second",
        out_shape=(struct((TILES * CELLS, CH), F32), struct(half, F32), struct(half, BF)),
        grid=(TILES,),
        in_specs=[
            smem(),
            smem(),
            per_tile(1, SIDE, SIDE, CH),
            per_tile(CELLS, CH),
            whole(got.shape),
            whole(triples.shape),
            whole(turned.shape),
        ],
        out_specs=(per_tile(CELLS, CH), whole(half), whole(half)),
        scratch_shapes=[
            pltpu.VMEM((CELLS + 2 * SIDE, 3 * CH), BF),
            pltpu.VMEM((CH, CELLS), BF),
            pltpu.VMEM((3, CH, 3 * CH), F32),
            pltpu.VMEM((TILES * SIDE, CH), BF),
        ],
        compiler_params=params(1),
        cost_estimate=cost(7_200_000_000, 12_000_000),
    )(routes, core, field, grad, got, triples, turned)


def first_kernel(
    routes_ref,
    core_ref,
    field_ref,
    cot_ref,
    back_ref,
    slope_ref,
    got_ref,
    returned_ref,
    kept_ref,
    given_ref,
    wide,
    across,
    total,
    flat,
    fresh,
    triples,
):
    tile = pl.program_id(0)

    @pl.when(tile == 0)
    def _():
        clear_margin(wide)
        total[...] = jnp.zeros_like(total)

    def one(i, carry):
        at = pl.ds(pl.multiple_of(i * SIDE, SIDE), SIDE)
        put(fresh, at, cot_ref[0, i].astype(F32) + back_ref[at, :])
        return carry

    lax.fori_loop(0, SIDE, one, 0, unroll=4)
    for edge in range(4):
        back = routes_ref[BACK + tile * 4 + edge]
        choose = pick(SIDE, lambda block: 0, back)
        rows = EDGE_ROWS[edge]
        add = dot(choose, returned_ref[routes_ref[GOT + tile * 4 + edge]])
        put(fresh, rows, take(fresh, rows) + add)

    def two(i, carry):
        at = pl.ds(pl.multiple_of(i * SIDE, SIDE), SIDE)
        put(fresh, at, take(fresh, at) * slope_ref[at, :].astype(F32))
        return carry

    lax.fori_loop(0, SIDE, two, 0, unroll=4)
    note_strips(fresh, triples, tile)
    spread(lambda i: take(fresh, pl.ds(pl.multiple_of(i * SIDE, SIDE), SIDE)), wide, False)
    outer(field_ref[0], wide, across, total)

    @pl.when(tile == TILES - 1)
    def _():
        outer_rims(routes_ref, got_ref, triples, total, flat)
        hand_over(core_ref[0], total, kept_ref, given_ref)


def first(routes, core, field, cotangent, back, slope, got, returned, pairs, depth):
    half = (pairs, 9, depth, CH)
    return pl.pallas_call(
        first_kernel,
        name="first",
        out_shape=(struct(half, F32), struct(half, BF)),
        grid=(TILES,),
        in_specs=[
            smem(),
            smem(),
            per_tile(1, SIDE, SIDE, CH),
            per_tile(1, SIDE, SIDE, CH),
            per_tile(CELLS, CH),
            per_tile(CELLS, CH),
            whole(got.shape),
            whole(returned.shape),
        ],
        out_specs=(whole(half), whole(half)),
        scratch_shapes=[
            pltpu.VMEM((CELLS + 2 * SIDE, 3 * CH), BF),
            pltpu.VMEM((CH, CELLS), BF),
            pltpu.VMEM((3, CH, 3 * CH), F32),
            pltpu.VMEM((TILES * SIDE, CH), BF),
            pltpu.VMEM((2, CELLS, 128), F32),
            pltpu.VMEM((4, TILES * SIDE, 3 * CH), BF),
        ],
        compiler_params=params(1),
        cost_estimate=cost(3_600_000_000, 12_000_000),
    )(routes, core, field, cotangent, back, slope, got, returned)


def cut_kernel(kept1_ref, got1_ref, kept2_ref, got2_ref, out_ref, rows):
    depth = kept1_ref.shape[2]
    run = 9 * depth // 4
    for layer, (kept_ref, got_ref) in enumerate(((kept1_ref, got1_ref), (kept2_ref, got2_ref))):
        for pair in range(kept_ref.shape[0]):
            for tap in range(9):
                rows[layer, pair, tap * depth : (tap + 1) * depth, :] = kept_ref[
                    pair, tap
                ] + got_ref[pair, tap].astype(F32)
            for peer in range(8):
                high, low = divmod(peer, 4)
                out_ref[pair * 8 + peer, layer * run : (layer + 1) * run, :] = rows[
                    layer, pair, low * run : (low + 1) * run, high * 128 : (high + 1) * 128
                ].astype(BF)


def cut(kept1, got1, kept2, got2):
    pairs, _, depth, _ = kept1.shape
    run = 9 * depth // 4
    return pl.pallas_call(
        cut_kernel,
        name="cut",
        out_shape=struct((pairs * 8, 2 * run, 128), BF),
        grid=(pairs // 2,),
        in_specs=[per_tile(2, 9, depth, CH)] * 4,
        out_specs=per_tile(16, 2 * run, 128),
        scratch_shapes=[pltpu.VMEM((2, 2, 9 * depth, CH), F32)],
        compiler_params=params(1),
        cost_estimate=cost(0, 6_000_000),
    )(kept1, got1, kept2, got2)


def sum_kernel(in_ref, out_ref):
    summed = in_ref[0].astype(F32)
    for other in range(1, in_ref.shape[0]):
        summed = summed + in_ref[other].astype(F32)
    for peer in range(out_ref.shape[0]):
        out_ref[peer] = summed.astype(BF)


def sum_all(parts, peers):
    return pl.pallas_call(
        sum_kernel,
        name="sum_all",
        out_shape=struct((peers, *parts.shape[1:]), BF),
        in_specs=[vmem()],
        out_specs=vmem(),
        compiler_params=params(),
        cost_estimate=cost(0, 2_000_000),
    )(parts)


def join_kernel(in_ref, out_ref):
    peers = in_ref.shape[0]
    run = in_ref.shape[1] // 2
    rows_all = out_ref.shape[0] // 2
    for layer in range(2):
        for peer in range(peers):
            high, low = divmod(peer, 4)
            at = layer * rows_all + low * run
            out_ref[at : at + run, high * 128 : (high + 1) * 128] = in_ref[
                peer, layer * run : (layer + 1) * run
            ].astype(F32)


def join(blocks, depth):
    return pl.pallas_call(
        join_kernel,
        name="join",
        out_shape=struct((2 * 9 * depth, CH), F32),
        in_specs=[vmem()],
        out_specs=vmem(),
        compiler_params=params(),
        cost_estimate=cost(0, 600_000),
    )(blocks)


def exchange(value, axes, groups=None):
    return lax.all_to_all(value, axes, 0, 0, tiled=True, axis_index_groups=groups)


def solution(mesh):
    shards, peers = mesh.shape["dp"], mesh.shape["space"]
    pairs, depth = shards // 2, CH // shards
    same_core_all = [
        [(pair * 2 + core) * peers + peer for pair in range(pairs) for peer in range(peers)]
        for core in range(2)
    ]
    swap = [(index, index ^ 1) for index in range(shards)]

    def gather(shard):
        blocks = []
        for step in range(1, pairs):
            route = [(index, index ^ (2 * step)) for index in range(shards)]
            blocks.append(lax.ppermute(shard, "dp", route))
        return blocks

    def trade(strips):
        return exchange(strips.reshape(peers, SLOTS, SIDE, CH), "space").reshape(strips.shape)

    def per_device(inputs, kernels, cotangent, adjacency):
        place = lax.axis_index("dp").astype(jnp.int32)
        core = jnp.stack([place % 2, place // 2])
        me = lax.axis_index("space").astype(jnp.int32).reshape(1)
        edges = exchange(jnp.broadcast_to(adjacency.reshape(1, 36), (peers, 36)), "space")
        blocks = gather(kernels.reshape(2, 9, depth, CH))
        field = inputs[0]
        cot = cotangent[0]
        send1, routes = pack(me, edges, field)
        own, send1 = lax.optimization_barrier((kernels.reshape(2, 9, depth, CH), send1))
        got1 = trade(send1)
        mine = jnp.stack([own, *blocks])
        theirs = lax.ppermute(mine, "dp", swap)
        part1, kernel1 = conv(core, field, mine, theirs, 0, False)
        state1, slope1, send2 = finish(routes, part1, field, got1, kernel1)
        got2 = trade(send2)
        part2, kernel2, turned2 = conv(core, state1, mine, theirs, 1, True)
        state2, grad2, send3, triples2 = last(routes, part2, state1, got2, kernel2, turned2, cot)
        returned = trade(send3)
        back, kept2, given2 = second(
            routes, core, state1, grad2, got2, triples2, turned2, pairs, depth
        )
        got_half2 = lax.ppermute(given2, "dp", swap)
        kept1, given1 = first(
            routes, core, field, cot, back, slope1, got1, returned, pairs, depth
        )
        blocks = cut(kept1, lax.ppermute(given1, "dp", swap), kept2, got_half2)
        summed = sum_all(exchange(blocks, ("dp", "space"), same_core_all), peers)
        grads = join(exchange(summed, "space"), depth)
        return state2[None], grads.reshape(2, 3, 3, depth, CH)

    in_specs = (
        P("dp", "space", None, None, None),
        P(None, None, None, "dp", None),
        P("dp", "space", None, None, None),
        P("space", None, None),
    )
    out_specs = (P("dp", "space", None, None, None), P(None, None, None, "dp", None))
    return jax.shard_map(
        per_device, mesh=mesh, in_specs=in_specs, out_specs=out_specs, check_vma=False
    )
```

```python
import jax
import jax.numpy as jnp
from jax import lax
from jax.experimental import pallas as pl
from jax.experimental.pallas import tpu as pltpu
from jax.sharding import PartitionSpec as P

BF = jnp.bfloat16
F32 = jnp.float32
TILES, SIDE, CH = 3, 32, 256
CELLS = SIDE * SIDE
SLOTS = 7
GOT, BACK = 64, 76


def vmem():
    return pl.BlockSpec(memory_space=pltpu.VMEM)


def smem():
    return pl.BlockSpec(memory_space=pltpu.SMEM)


def whole(shape):
    zeros = (0,) * len(shape)
    return pl.BlockSpec(shape, lambda t: zeros)


def per_tile(*tail):
    zeros = (0,) * (len(tail) - 1)
    return pl.BlockSpec(tail, lambda t: (t, *zeros))


def struct(shape, dtype):
    return jax.ShapeDtypeStruct(shape, dtype)


def params(steps=0):
    if steps:
        return pltpu.CompilerParams(
            dimension_semantics=("arbitrary",), vmem_limit_bytes=60 * 1024 * 1024
        )
    return pltpu.CompilerParams(vmem_limit_bytes=60 * 1024 * 1024)


def cost(flops, moved):
    return pl.CostEstimate(flops=flops, bytes_accessed=moved, transcendentals=0)


def take(halves, rows):
    return jnp.concatenate([halves[0, rows, :], halves[1, rows, :]], axis=1)


def put(halves, rows, value):
    halves[0, rows, :] = value[:, 0:128]
    halves[1, rows, :] = value[:, 128:256]


def fill(routes_ref, strips, send_ref):
    for slot in range(send_ref.shape[0]):
        send_ref[slot] = strips[routes_ref[slot]]


def pack_kernel(me_ref, adj_ref, field_ref, send_ref, routes_ref, column, strips):
    peers = adj_ref.shape[0]
    me = me_ref[0]
    for slot in range(GOT):
        routes_ref[slot] = 0
    for peer in range(peers):
        sent = jnp.int32(0)
        for edge in range(4 * TILES):
            other = adj_ref[peer, edge * 3]
            owner = lax.div(other, TILES)
            mine = (owner == me).astype(jnp.int32)
            slot = peer * SLOTS + jnp.minimum(sent, SLOTS - 1)
            strip = (other - owner * TILES) * 4 + adj_ref[peer, edge * 3 + 1]
            routes_ref[jnp.where(owner == me, slot, GOT - 1)] = jnp.where(owner == me, strip, 0)
            sent += mine
    owners = []
    for edge in range(4 * TILES):
        owners.append(lax.div(adj_ref[me, edge * 3], TILES))
        before = jnp.int32(0)
        for there in range(edge):
            before += (owners[there] == owners[edge]).astype(jnp.int32)
        routes_ref[GOT + edge] = owners[edge] * SLOTS + jnp.minimum(before, SLOTS - 1)
        routes_ref[BACK + edge] = adj_ref[me, edge * 3 + 2]
    for tile in range(TILES):
        strips[tile * 4] = field_ref[tile, 0]
        strips[tile * 4 + 1] = field_ref[tile, SIDE - 1]
        for edge, first, lane in ((2, 0, 0), (3, SIDE - 8, 7)):
            near = field_ref[tile, :, first : first + 8].astype(F32).reshape(SIDE * 8, CH)
            put(column, slice(None), near)
            strips[tile * 4 + edge] = take(column, pl.ds(lane, SIDE, stride=8)).astype(BF)
    fill(routes_ref, strips, send_ref)


def pack(me, adjacency, field):
    peers = adjacency.shape[0]
    return pl.pallas_call(
        pack_kernel,
        name="pack",
        out_shape=(struct((peers * SLOTS, SIDE, CH), BF), struct((BACK + 12,), jnp.int32)),
        in_specs=[smem(), smem(), vmem()],
        out_specs=(vmem(), smem()),
        scratch_shapes=[
            pltpu.VMEM((2, SIDE * 8, 128), F32),
            pltpu.VMEM((4 * TILES, SIDE, CH), BF),
        ],
        compiler_params=params(),
        cost_estimate=cost(0, 3_000_000),
    )(me, adjacency, field)


def pick(rows, shift_of_block, backwards):
    row = lax.broadcasted_iota(jnp.int32, (rows, SIDE), 0)
    cell = lax.broadcasted_iota(jnp.int32, (rows, SIDE), 1)
    block = row // SIDE
    place = row - block * SIDE
    source = place + shift_of_block(block)
    inside = (source >= 0) & (source < SIDE)
    if backwards is not None:
        source = jnp.where(backwards == 1, SIDE - 1 - source, source)
    return jnp.where(inside & (cell == source), 1.0, 0.0).astype(BF)


def dot(left, right):
    return jnp.dot(left, right, preferred_element_type=F32)


def dot_rows(left, right):
    return lax.dot_general(left, right, (((0,), (0,)), ((), ())), preferred_element_type=F32)


def block_of_edge(edge, k):
    return (k, 6 + k, 3 * k, 3 * k + 2)[edge]


EDGE_ROWS = (
    pl.ds(0, SIDE),
    pl.ds(CELLS - SIDE, SIDE),
    pl.ds(0, SIDE, stride=SIDE),
    pl.ds(SIDE - 1, SIDE, stride=SIDE),
)


def spread(source, out_ref, ascending):
    first = lax.broadcasted_iota(jnp.int32, (SIDE, CH), 0) == 0
    last = lax.broadcasted_iota(jnp.int32, (SIDE, CH), 0) == SIDE - 1

    def one(i, carry):
        row = source(i).astype(F32)
        earlier = jnp.where(first, 0.0, pltpu.roll(row, 1, 0)).astype(BF)
        later = jnp.where(last, 0.0, pltpu.roll(row, SIDE - 1, 0)).astype(BF)
        at = pl.ds(pl.multiple_of((i + 1) * SIDE, SIDE), SIDE)
        low, high = (earlier, later) if ascending else (later, earlier)
        out_ref[at, 0:CH] = low
        out_ref[at, CH : 2 * CH] = row.astype(BF)
        out_ref[at, 2 * CH : 3 * CH] = high
        return carry

    lax.fori_loop(0, SIDE, one, 0, unroll=4)


def clear_margin(out_ref):
    zero = jnp.zeros((SIDE, 3 * CH), BF)
    out_ref[0:SIDE, :] = zero
    out_ref[CELLS + SIDE : CELLS + 2 * SIDE, :] = zero


def conv_kernel(turned, shards, core_ref, field_ref, mine_ref, theirs_ref, *refs):
    if turned:
        part_ref, kernel_ref, turned_ref, wide = refs
    else:
        part_ref, kernel_ref, wide = refs
    depth = CH // shards
    core = core_ref[0]

    @pl.when(pl.program_id(0) == 0)
    def _():
        clear_margin(wide)
        for pair in range(shards // 2):
            for source, side in ((mine_ref, core), (theirs_ref, 1 - core)):
                base = (core_ref[1] ^ pair) * 2 * depth + side * depth
                for tap in range(9):
                    at = pl.multiple_of(tap * CH + base, depth)
                    kernel_ref[pl.ds(at, depth), :] = source[pair, 0, tap]
        if turned:
            for tap in range(9):
                turned_ref[tap * CH : (tap + 1) * CH, :] = kernel_ref[tap * CH : (tap + 1) * CH, :].T

    spread(lambda i: field_ref[0, i], wide, True)

    def chunk(c, carry):
        total = None
        for p in range(3):
            at = pl.multiple_of(c * CH + p * SIDE, SIDE)
            term = dot(wide[pl.ds(at, CH), :], kernel_ref[p * 3 * CH : (p + 1) * 3 * CH, :])
            total = term if total is None else total + term
        part_ref[pl.ds(pl.multiple_of(c * CH, CH), CH), :] = total
        return carry

    lax.fori_loop(0, CELLS // CH, chunk, 0)


def conv(core, field, mine, theirs, layer, turned):
    pieces = pl.BlockSpec((mine.shape[0], 1, *mine.shape[2:]), lambda t: (0, layer, 0, 0, 0))
    shards = mine.shape[0] * 2
    outs = [struct((TILES * CELLS, CH), F32), struct((9 * CH, CH), BF)]
    specs = [per_tile(CELLS, CH), whole((9 * CH, CH))]
    if turned:
        outs.append(struct((9 * CH, CH), BF))
        specs.append(whole((9 * CH, CH)))
    return pl.pallas_call(
        lambda *refs: conv_kernel(turned, shards, *refs),
        name="conv_turned" if turned else "conv",
        out_shape=tuple(outs),
        grid=(TILES,),
        in_specs=[smem(), per_tile(1, SIDE, SIDE, CH), pieces, pieces],
        out_specs=tuple(specs),
        scratch_shapes=[pltpu.VMEM((CELLS + 2 * SIDE, 3 * CH), BF)],
        compiler_params=params(1),
        cost_estimate=cost(3_600_000_000, 7_000_000),
    )(core, field, mine, theirs)


def add_rims(routes_ref, got_ref, kernel_ref, rows3, rim_part):
    for edge in range(4):
        for tile in range(TILES):
            back = routes_ref[BACK + tile * 4 + edge]
            choose = pick(3 * SIDE, lambda block: block - 1, back)
            shifted = dot(choose, got_ref[routes_ref[GOT + tile * 4 + edge]]).astype(BF)
            for k in range(3):
                rows3[tile * SIDE : (tile + 1) * SIDE, k * CH : (k + 1) * CH] = shifted[
                    k * SIDE : (k + 1) * SIDE
                ]
        total = None
        for k in range(3):
            block = block_of_edge(edge, k)
            term = dot(
                rows3[:, k * CH : (k + 1) * CH], kernel_ref[block * CH : (block + 1) * CH, :]
            )
            total = term if total is None else total + term
        rim_part[edge] = total


def with_rims(part_ref, rim_part, out):
    tile = pl.program_id(0)
    put(out, slice(None), part_ref[...])
    for edge in range(4):
        rows = EDGE_ROWS[edge]
        add = rim_part[edge, pl.ds(pl.multiple_of(tile * SIDE, SIDE), SIDE), :]
        put(out, rows, take(out, rows) + add)


def finish_kernel(
    routes_ref,
    part_ref,
    field_ref,
    got_ref,
    kernel_ref,
    state_ref,
    slope_ref,
    send_ref,
    rows3,
    rim_part,
    fresh,
    strips,
):
    tile = pl.program_id(0)

    @pl.when(tile == 0)
    def _():
        add_rims(routes_ref, got_ref, kernel_ref, rows3, rim_part)

    with_rims(part_ref, rim_part, fresh)

    def one(i, carry):
        at = pl.ds(pl.multiple_of(i * SIDE, SIDE), SIDE)
        v = take(fresh, at)
        s = 1.0 / (1.0 + jnp.exp(-v))
        updated = field_ref[0, i].astype(F32) + v * s
        put(fresh, at, updated)
        state_ref[0, i] = updated.astype(BF)
        slope_ref[at, :] = (s * (1.0 + v * (1.0 - s))).astype(BF)
        return carry

    lax.fori_loop(0, SIDE, one, 0, unroll=4)
    for edge in range(4):
        strips[tile * 4 + edge] = take(fresh, EDGE_ROWS[edge]).astype(BF)

    @pl.when(tile == TILES - 1)
    def _():
        fill(routes_ref, strips, send_ref)


def finish(routes, part, field, got, kernel):
    return pl.pallas_call(
        finish_kernel,
        name="finish",
        out_shape=(
            struct(field.shape, BF),
            struct(part.shape, BF),
            struct(got.shape, BF),
        ),
        grid=(TILES,),
        in_specs=[
            smem(),
            per_tile(CELLS, CH),
            per_tile(1, SIDE, SIDE, CH),
            whole(got.shape),
            whole(kernel.shape),
        ],
        out_specs=(per_tile(1, SIDE, SIDE, CH), per_tile(CELLS, CH), whole(got.shape)),
        scratch_shapes=[
            pltpu.VMEM((TILES * SIDE, 3 * CH), BF),
            pltpu.VMEM((4, TILES * SIDE, CH), F32),
            pltpu.VMEM((2, CELLS, 128), F32),
            pltpu.VMEM((4 * TILES, SIDE, CH), BF),
        ],
        compiler_params=params(1),
        cost_estimate=cost(200_000_000, 10_000_000),
    )(routes, part, field, got, kernel)


def note_strips(grad, triples, tile):
    choose = pick(3 * SIDE, lambda block: 1 - block, None)
    for edge in range(4):
        shifted = dot(choose, take(grad, EDGE_ROWS[edge]).astype(BF)).astype(BF)
        for k in range(3):
            triples[
                edge, pl.ds(pl.multiple_of(tile * SIDE, SIDE), SIDE), k * CH : (k + 1) * CH
            ] = shifted[k * SIDE : (k + 1) * SIDE]


def last_kernel(
    routes_ref,
    part_ref,
    field_ref,
    got_ref,
    kernel_ref,
    turned_ref,
    cot_ref,
    state_ref,
    grad_ref,
    send_ref,
    triples_ref,
    rows3,
    rim_part,
    fresh,
    strips,
):
    tile = pl.program_id(0)

    @pl.when(tile == 0)
    def _():
        add_rims(routes_ref, got_ref, kernel_ref, rows3, rim_part)

    with_rims(part_ref, rim_part, fresh)

    def one(i, carry):
        at = pl.ds(pl.multiple_of(i * SIDE, SIDE), SIDE)
        v = take(fresh, at)
        s = 1.0 / (1.0 + jnp.exp(-v))
        state_ref[0, i] = (field_ref[0, i].astype(F32) + v * s).astype(BF)
        grad = cot_ref[0, i].astype(F32) * s * (1.0 + v * (1.0 - s))
        put(fresh, at, grad)
        grad_ref[at, :] = grad.astype(BF)
        return carry

    lax.fori_loop(0, SIDE, one, 0, unroll=4)
    note_strips(fresh, triples_ref, tile)

    @pl.when(tile == TILES - 1)
    def _():
        for edge in range(4):
            total = None
            for k in range(3):
                block = block_of_edge(edge, k)
                term = dot(
                    triples_ref[edge, :, k * CH : (k + 1) * CH],
                    turned_ref[block * CH : (block + 1) * CH, :],
                )
                total = term if total is None else total + term
            for there in range(TILES):
                strips[there * 4 + edge] = total[there * SIDE : (there + 1) * SIDE].astype(BF)
        fill(routes_ref, strips, send_ref)


def last(routes, part, field, got, kernel, turned, cotangent):
    triples = (4, TILES * SIDE, 3 * CH)
    return pl.pallas_call(
        last_kernel,
        name="last",
        out_shape=(
            struct(field.shape, BF),
            struct((TILES * CELLS, CH), BF),
            struct(got.shape, BF),
            struct(triples, BF),
        ),
        grid=(TILES,),
        in_specs=[
            smem(),
            per_tile(CELLS, CH),
            per_tile(1, SIDE, SIDE, CH),
            whole(got.shape),
            whole(kernel.shape),
            whole(turned.shape),
            per_tile(1, SIDE, SIDE, CH),
        ],
        out_specs=(
            per_tile(1, SIDE, SIDE, CH),
            per_tile(CELLS, CH),
            whole(got.shape),
            whole(triples),
        ),
        scratch_shapes=[
            pltpu.VMEM((TILES * SIDE, 3 * CH), BF),
            pltpu.VMEM((4, TILES * SIDE, CH), F32),
            pltpu.VMEM((2, CELLS, 128), F32),
            pltpu.VMEM((4 * TILES, SIDE, CH), BF),
        ],
        compiler_params=params(1),
        cost_estimate=cost(400_000_000, 12_000_000),
    )(routes, part, field, got, kernel, turned, cotangent)


def outer(field, wide, across, total):
    across[...] = field.reshape(CELLS, CH).T

    def one(p, carry):
        at = pl.multiple_of((2 - p) * SIDE, SIDE)
        total[p] = total[p] + dot(across[...], wide[pl.ds(at, CELLS), :])
        return carry

    lax.fori_loop(0, 3, one, 0)


def outer_rims(routes_ref, got_ref, triples, total, flat):
    for edge in range(4):
        for tile in range(TILES):
            back = routes_ref[BACK + tile * 4 + edge]
            choose = pick(SIDE, lambda block: 0, back)
            flat[tile * SIDE : (tile + 1) * SIDE, :] = dot(
                choose, got_ref[routes_ref[GOT + tile * 4 + edge]]
            ).astype(BF)
        for k in range(3):
            p, q = divmod(block_of_edge(edge, k), 3)
            lanes = slice(q * CH, (q + 1) * CH)
            total[p, :, lanes] = total[p, :, lanes] + dot_rows(
                flat[...], triples[edge, :, k * CH : (k + 1) * CH]
            )


def hand_over(core, total, kept_ref, given_ref):
    pairs = kept_ref.shape[0]
    depth = kept_ref.shape[2]
    for pair in range(pairs):
        own = pl.ds(pl.multiple_of(pair * 2 * depth + core * depth, depth), depth)
        other = pl.ds(pl.multiple_of(pair * 2 * depth + (1 - core) * depth, depth), depth)
        for tap in range(9):
            p, q = divmod(tap, 3)
            kept_ref[pair, tap] = total[p, own, q * CH : (q + 1) * CH]
            given_ref[pair, tap] = total[p, other, q * CH : (q + 1) * CH].astype(BF)


def second_kernel(
    routes_ref,
    core_ref,
    field_ref,
    grad_ref,
    got_ref,
    triples_ref,
    turned_ref,
    back_ref,
    kept_ref,
    given_ref,
    wide,
    across,
    total,
    flat,
):
    tile = pl.program_id(0)

    @pl.when(tile == 0)
    def _():
        clear_margin(wide)
        total[...] = jnp.zeros_like(total)

    spread(lambda i: grad_ref[pl.ds(pl.multiple_of(i * SIDE, SIDE), SIDE), :], wide, False)

    def chunk(c, carry):
        result = None
        for p in range(3):
            at = pl.multiple_of(c * CH + (2 - p) * SIDE, SIDE)
            term = dot(wide[pl.ds(at, CH), :], turned_ref[p * 3 * CH : (p + 1) * 3 * CH, :])
            result = term if result is None else result + term
        back_ref[pl.ds(pl.multiple_of(c * CH, CH), CH), :] = result
        return carry

    lax.fori_loop(0, CELLS // CH, chunk, 0)
    outer(field_ref[0], wide, across, total)

    @pl.when(tile == TILES - 1)
    def _():
        outer_rims(routes_ref, got_ref, triples_ref, total, flat)
        hand_over(core_ref[0], total, kept_ref, given_ref)


def second(routes, core, field, grad, got, triples, turned, pairs, depth):
    half = (pairs, 9, depth, CH)
    return pl.pallas_call(
        second_kernel,
        name="second",
        out_shape=(struct((TILES * CELLS, CH), F32), struct(half, F32), struct(half, BF)),
        grid=(TILES,),
        in_specs=[
            smem(),
            smem(),
            per_tile(1, SIDE, SIDE, CH),
            per_tile(CELLS, CH),
            whole(got.shape),
            whole(triples.shape),
            whole(turned.shape),
        ],
        out_specs=(per_tile(CELLS, CH), whole(half), whole(half)),
        scratch_shapes=[
            pltpu.VMEM((CELLS + 2 * SIDE, 3 * CH), BF),
            pltpu.VMEM((CH, CELLS), BF),
            pltpu.VMEM((3, CH, 3 * CH), F32),
            pltpu.VMEM((TILES * SIDE, CH), BF),
        ],
        compiler_params=params(1),
        cost_estimate=cost(7_200_000_000, 12_000_000),
    )(routes, core, field, grad, got, triples, turned)


def first_kernel(
    routes_ref,
    core_ref,
    field_ref,
    cot_ref,
    back_ref,
    slope_ref,
    got_ref,
    returned_ref,
    kept_ref,
    given_ref,
    wide,
    across,
    total,
    flat,
    fresh,
    triples,
):
    tile = pl.program_id(0)

    @pl.when(tile == 0)
    def _():
        clear_margin(wide)
        total[...] = jnp.zeros_like(total)

    def one(i, carry):
        at = pl.ds(pl.multiple_of(i * SIDE, SIDE), SIDE)
        put(fresh, at, cot_ref[0, i].astype(F32) + back_ref[at, :])
        return carry

    lax.fori_loop(0, SIDE, one, 0, unroll=4)
    for edge in range(4):
        back = routes_ref[BACK + tile * 4 + edge]
        choose = pick(SIDE, lambda block: 0, back)
        rows = EDGE_ROWS[edge]
        add = dot(choose, returned_ref[routes_ref[GOT + tile * 4 + edge]])
        put(fresh, rows, take(fresh, rows) + add)

    def two(i, carry):
        at = pl.ds(pl.multiple_of(i * SIDE, SIDE), SIDE)
        put(fresh, at, take(fresh, at) * slope_ref[at, :].astype(F32))
        return carry

    lax.fori_loop(0, SIDE, two, 0, unroll=4)
    note_strips(fresh, triples, tile)
    spread(lambda i: take(fresh, pl.ds(pl.multiple_of(i * SIDE, SIDE), SIDE)), wide, False)
    outer(field_ref[0], wide, across, total)

    @pl.when(tile == TILES - 1)
    def _():
        outer_rims(routes_ref, got_ref, triples, total, flat)
        hand_over(core_ref[0], total, kept_ref, given_ref)


def first(routes, core, field, cotangent, back, slope, got, returned, pairs, depth):
    half = (pairs, 9, depth, CH)
    return pl.pallas_call(
        first_kernel,
        name="first",
        out_shape=(struct(half, F32), struct(half, BF)),
        grid=(TILES,),
        in_specs=[
            smem(),
            smem(),
            per_tile(1, SIDE, SIDE, CH),
            per_tile(1, SIDE, SIDE, CH),
            per_tile(CELLS, CH),
            per_tile(CELLS, CH),
            whole(got.shape),
            whole(returned.shape),
        ],
        out_specs=(whole(half), whole(half)),
        scratch_shapes=[
            pltpu.VMEM((CELLS + 2 * SIDE, 3 * CH), BF),
            pltpu.VMEM((CH, CELLS), BF),
            pltpu.VMEM((3, CH, 3 * CH), F32),
            pltpu.VMEM((TILES * SIDE, CH), BF),
            pltpu.VMEM((2, CELLS, 128), F32),
            pltpu.VMEM((4, TILES * SIDE, 3 * CH), BF),
        ],
        compiler_params=params(1),
        cost_estimate=cost(3_600_000_000, 12_000_000),
    )(routes, core, field, cotangent, back, slope, got, returned)


def cut_kernel(kept1_ref, got1_ref, kept2_ref, got2_ref, out_ref, rows):
    depth = kept1_ref.shape[2]
    run = 9 * depth // 4
    for layer, (kept_ref, got_ref) in enumerate(((kept1_ref, got1_ref), (kept2_ref, got2_ref))):
        for pair in range(kept_ref.shape[0]):
            for tap in range(9):
                rows[layer, pair, tap * depth : (tap + 1) * depth, :] = kept_ref[
                    pair, tap
                ] + got_ref[pair, tap].astype(F32)
            for peer in range(8):
                high, low = divmod(peer, 4)
                out_ref[pair * 8 + peer, layer * run : (layer + 1) * run, :] = rows[
                    layer, pair, low * run : (low + 1) * run, high * 128 : (high + 1) * 128
                ].astype(BF)


def cut(kept1, got1, kept2, got2):
    pairs, _, depth, _ = kept1.shape
    run = 9 * depth // 4
    return pl.pallas_call(
        cut_kernel,
        name="cut",
        out_shape=struct((pairs * 8, 2 * run, 128), BF),
        grid=(pairs // 2,),
        in_specs=[per_tile(2, 9, depth, CH)] * 4,
        out_specs=per_tile(16, 2 * run, 128),
        scratch_shapes=[pltpu.VMEM((2, 2, 9 * depth, CH), F32)],
        compiler_params=params(1),
        cost_estimate=cost(0, 6_000_000),
    )(kept1, got1, kept2, got2)


def sum_kernel(in_ref, out_ref):
    summed = in_ref[0].astype(F32)
    for other in range(1, in_ref.shape[0]):
        summed = summed + in_ref[other].astype(F32)
    for peer in range(out_ref.shape[0]):
        out_ref[peer] = summed.astype(BF)


def sum_all(parts, peers):
    return pl.pallas_call(
        sum_kernel,
        name="sum_all",
        out_shape=struct((peers, *parts.shape[1:]), BF),
        in_specs=[vmem()],
        out_specs=vmem(),
        compiler_params=params(),
        cost_estimate=cost(0, 2_000_000),
    )(parts)


def join_kernel(in_ref, out_ref):
    peers = in_ref.shape[0]
    run = in_ref.shape[1] // 2
    rows_all = out_ref.shape[0] // 2
    for layer in range(2):
        for peer in range(peers):
            high, low = divmod(peer, 4)
            at = layer * rows_all + low * run
            out_ref[at : at + run, high * 128 : (high + 1) * 128] = in_ref[
                peer, layer * run : (layer + 1) * run
            ].astype(F32)


def join(blocks, depth):
    return pl.pallas_call(
        join_kernel,
        name="join",
        out_shape=struct((2 * 9 * depth, CH), F32),
        in_specs=[vmem()],
        out_specs=vmem(),
        compiler_params=params(),
        cost_estimate=cost(0, 600_000),
    )(blocks)


def exchange(value, axes, groups=None):
    return lax.all_to_all(value, axes, 0, 0, tiled=True, axis_index_groups=groups)


def solution(mesh):
    shards, peers = mesh.shape["dp"], mesh.shape["space"]
    pairs, depth = shards // 2, CH // shards
    same_core_all = [
        [(pair * 2 + core) * peers + peer for pair in range(pairs) for peer in range(peers)]
        for core in range(2)
    ]
    swap = [(index, index ^ 1) for index in range(shards)]

    def gather(shard):
        blocks = []
        for step in range(1, pairs):
            route = [(index, index ^ (2 * step)) for index in range(shards)]
            blocks.append(lax.ppermute(shard, "dp", route))
        return blocks

    def trade(strips):
        return exchange(strips.reshape(peers, SLOTS, SIDE, CH), "space").reshape(strips.shape)

    def per_device(inputs, kernels, cotangent, adjacency):
        place = lax.axis_index("dp").astype(jnp.int32)
        core = jnp.stack([place % 2, place // 2])
        me = lax.axis_index("space").astype(jnp.int32).reshape(1)
        edges = exchange(jnp.broadcast_to(adjacency.reshape(1, 36), (peers, 36)), "space")
        blocks = gather(kernels.reshape(2, 9, depth, CH))
        field = inputs[0]
        cot = cotangent[0]
        send1, routes = pack(me, edges, field)
        own, send1 = lax.optimization_barrier((kernels.reshape(2, 9, depth, CH), send1))
        got1 = trade(send1)
        mine = jnp.stack([own, *blocks])
        theirs = lax.ppermute(mine, "dp", swap)
        part1, kernel1 = conv(core, field, mine, theirs, 0, False)
        state1, slope1, send2 = finish(routes, part1, field, got1, kernel1)
        got2 = trade(send2)
        part2, kernel2, turned2 = conv(core, state1, mine, theirs, 1, True)
        state2, grad2, send3, triples2 = last(routes, part2, state1, got2, kernel2, turned2, cot)
        returned = trade(send3)
        back, kept2, given2 = second(
            routes, core, state1, grad2, got2, triples2, turned2, pairs, depth
        )
        got_half2 = lax.ppermute(given2, "dp", swap)
        kept1, given1 = first(
            routes, core, field, cot, back, slope1, got1, returned, pairs, depth
        )
        blocks = cut(kept1, lax.ppermute(given1, "dp", swap), kept2, got_half2)
        summed = sum_all(exchange(blocks, ("dp", "space"), same_core_all), peers)
        grads = join(exchange(summed, "space"), depth)
        return state2[None], grads.reshape(2, 3, 3, depth, CH)

    in_specs = (
        P("dp", "space", None, None, None),
        P(None, None, None, "dp", None),
        P("dp", "space", None, None, None),
        P("space", None, None),
    )
    out_specs = (P("dp", "space", None, None, None), P(None, None, None, "dp", None))
    return jax.shard_map(
        per_device, mesh=mesh, in_specs=in_specs, out_specs=out_specs, check_vma=False
    )
```
